32 devices in a mesh: seq: 4 (over x, core), exp: 8 (over z, y).
Axes of the slice: x: 2, y: 2, z: 4, core: 2. Of those that a mesh axis runs over, the one named last changes fastest.
Arguments:
- residual_in: bfloat16 [4096, 2048], P(('seq', 'exp')), may hold values from -8 to 8
- ssm_input: bfloat16 [4096, 2048], P(('seq', 'exp')), may hold values from -6 to 6
- ssm_b: bfloat16 [4096, 128], P(('seq', 'exp')), may hold values from -6 to 6
- ssm_c: bfloat16 [4096, 128], P(('seq', 'exp')), may hold values from -0.5 to 0.5
- log_decay: float32 [4096, 32], P(('seq', 'exp')), may hold values from -2 to 0, as said below
- skip_gain: float32 [32], replicated, may hold values from 0.5 to 1.5
- out_proj: bfloat16 [2048, 2048], replicated, may hold values from -0.125 to 0.125
- norm_gain: float32 [2048], replicated, may hold values from 0.5 to 1.5
- router: bfloat16 [2048, 16], replicated, may hold values from -1 to 1
- assignment: int32 [4096, 1], P(('seq', 'exp')), may hold values from 0 to 15; in each aligned block of 128 rows (0 to 127, 128 to 255, ...) at most 16 rows name the same one
- expert_gate: bfloat16 [32, 2048, 704], P(('seq', 'exp')), may hold values from -0.125 to 0.125
- expert_up: bfloat16 [32, 2048, 704], P(('seq', 'exp')), may hold values from -0.125 to 0.125
- expert_down: bfloat16 [32, 704, 2048], P(('seq', 'exp')), may hold values from -0.15625 to 0.15625
Outputs:
- layer_out: bfloat16 [4096, 2048], P(('seq', 'exp'))
- route_weight: float32 [4096], P(('seq', 'exp'))
The draws below stay inside these ranges and needn't reach their ends.
Inputs may be any that keep to these rules, and one draw needn't show every extreme that they name: `log_decay`: every entry is negative. `assignment`: on the rows of one device no expert is named more than 16 times; in every draw some expert is named exactly 16 times on some device.
All inputs are finite; a program needn't handle non-finite values.
Results may differ from the reference program's by a relative error of at most 0.009.
Values may be sent and summed in bfloat16 or wider, within the bound.
A program may use at most 576 MiB of HBM per device.

```python
import math
import jax
import jax.numpy as jnp
import numpy as np
from jax import lax

D = 2048
MIXER_HEADS = 32
HEAD_DIM = 64
STATE = 128
FF = 1408
BLOCK = 128
SINK_ITERS = 8
TOK_DEV = 128
EXPERTS = 16
CAPACITY = 16
SEQUENCE_TOKENS = 4096
N_SEQ = 4
N_EXP = 8


def draw_log_decay(key, part):
    random_subkeys = jax.random.split(key, 7)
    slow_count = max(1, MIXER_HEADS // 2)
    head_order = jax.random.permutation(random_subkeys[0], MIXER_HEADS)
    slow_heads = head_order < slow_count
    slow_rate = jnp.exp(jax.random.uniform(random_subkeys[1], (MIXER_HEADS,), jnp.float32, -2.5, -0.5)) / SEQUENCE_TOKENS
    fast_rate = jnp.exp(jax.random.uniform(random_subkeys[2], (MIXER_HEADS,), jnp.float32, -0.25, 0.25)) / 40.0
    head_decay_rate = jnp.where(slow_heads, slow_rate, fast_rate)
    token_factor = jnp.exp(jax.random.uniform(random_subkeys[3], (SEQUENCE_TOKENS // TOK_DEV, TOK_DEV, MIXER_HEADS), jnp.float32, -0.7, 0.7))
    block_factor = jnp.exp(jax.random.uniform(random_subkeys[4], (SEQUENCE_TOKENS // TOK_DEV, 1, MIXER_HEADS), jnp.float32, -0.35, 0.35))
    scale_multiplier = (token_factor * block_factor).reshape(SEQUENCE_TOKENS, MIXER_HEADS)
    spike_location = jax.random.randint(random_subkeys[5], (2,), 0, SEQUENCE_TOKENS)
    spike_depth = jax.random.uniform(random_subkeys[6], (2, MIXER_HEADS), jnp.float32, 0.2, 0.5)
    token_positions = jnp.arange(SEQUENCE_TOKENS)
    spike_start_token = (token_positions[:, None] == spike_location[0]).astype(jnp.float32) * (-jnp.log(1.0 - spike_depth[0]))[None, :]
    spike_second_token = (token_positions[:, None] == spike_location[1]).astype(jnp.float32) * (-jnp.log(1.0 - spike_depth[1]))[None, :]
    return -(head_decay_rate[None, :] * scale_multiplier) - spike_start_token - spike_second_token


def cluster_sides(key):
    base_key = jax.random.fold_in(key, 7919)
    random_subkeys = jax.random.split(base_key, 3)
    direction = jnp.where(jax.random.bernoulli(random_subkeys[0], 0.5, (D,)), 1.0, -1.0).astype(jnp.float32)
    share_start = 0.3
    share_end = 0.86
    placing = jnp.arange(SEQUENCE_TOKENS).astype(jnp.float32) / SEQUENCE_TOKENS
    share = share_start + (share_end - share_start) * placing
    token_side = jnp.where(jax.random.bernoulli(random_subkeys[1], share), 1.0, -1.0).astype(jnp.float32)
    expert_side = jnp.where(jax.random.permutation(random_subkeys[2], EXPERTS) < EXPERTS // 2, 1.0, -1.0).astype(jnp.float32)
    return (direction, token_side, expert_side)


def draw_residual_in(key, part):
    direction, token_side, expert_side = cluster_sides(key)
    spread_key = jax.random.fold_in(key, 104729)
    random_part = jax.random.truncated_normal(spread_key, -6.0, 6.0, (SEQUENCE_TOKENS, D), jnp.float32)
    strength = 1.0
    return (random_part + strength * token_side[:, None] * direction[None, :]).astype(jnp.bfloat16)


def draw_router(key, part):
    direction, token_side, expert_side = cluster_sides(key)
    spread_key = jax.random.fold_in(key, 15485863)
    random_part = jax.random.truncated_normal(spread_key, -6.0, 6.0, (D, EXPERTS), jnp.float32)
    return (random_part * D ** (-0.5) + 4.5 / D * direction[:, None] * expert_side[None, :]).astype(jnp.bfloat16)


def levels(stream_key, dims, cuts, least, top_value):
    gain = 1.0
    for dim, blocks in cuts:
        heights = jax.random.uniform(jax.random.fold_in(jax.random.fold_in(stream_key, 6), dim), (blocks,), jnp.float32, least / len(cuts), top_value / len(cuts))
        gain = gain * jnp.repeat(jnp.exp(heights), dims[dim] // blocks).reshape((-1,) + (1,) * (len(dims) - 1 - dim))
    return gain


def assign_block(rng, own, number, rows, count, top, most, lean):
    sequence = jax.random.permutation(rng, count)
    crowded, ordinary = portions_of(count, rows * top, most, lean, True), portions_of(count, rows * top, most, lean, False)
    places = jnp.arange(count)

    def named(lengths, turn):
        used = int((lengths > 0).sum())
        fixed = max(1, used // 4)
        passed = fixed + (places - fixed + turn * (used - fixed)) % max(1, count - fixed)
        return jnp.zeros((count,), jnp.int32).at[sequence[jnp.where(places < fixed, places, passed)]].set(jnp.asarray(lengths, jnp.int32))

    lengths = jnp.where(number % 4 == 0, named(crowded, number // 4), named(ordinary, number - number // 4 - 1))
    mixed = jax.random.permutation(jax.random.fold_in(own, 3), count)
    giver, sink = mixed[0:count // 2 * 2:2], mixed[1:count // 2 * 2:2]
    room = jnp.minimum(lengths[giver] - 1, most - lengths[sink]) // 2
    room = jnp.where((giver == sequence[0]) | (sink == sequence[0]) | (lengths[sink] == 0), 0, jnp.maximum(room, 0))
    passed = jax.random.randint(jax.random.fold_in(own, 4), (count // 2,), 0, 1 << 20) % (room + 1)
    lengths = lengths.at[giver].add(-passed).at[sink].add(passed)
    labels = jnp.searchsorted(jnp.cumsum(lengths), jnp.arange(rows * top), side="right").astype(jnp.int32)
    grid = labels.reshape(top, rows).T
    grid = grid[jax.random.permutation(jax.random.fold_in(own, 1), rows)]
    turn = jax.random.randint(jax.random.fold_in(own, 2), (rows, 1), 0, top)
    return jnp.take_along_axis(grid, (jnp.arange(top)[None, :] + turn) % top, axis=1)


def portions_of(amount, total, bound, slope, full):
    weights = [(1 << 20) // math.isqrt(rank ** slope) + 1 for rank in range(1, amount + 1)]
    largest = bound if full else min(bound, max(-(-total // amount), total * weights[0] // sum(weights)))
    least = 1 if total - largest >= amount - 1 else 0
    given, spare = [largest] + [least] * (amount - 1), total - largest - least * (amount - 1)
    while spare > 0:
        movable = [i for i in range(1, amount) if given[i] < largest] or [i for i in range(1, amount) if given[i] < bound]
        mass, remaining = sum([weights[i] for i in movable]), spare
        for i in movable:
            more = min(bound - given[i], max(1, remaining * weights[i] // mass), spare)
            given[i] = given[i] + more
            spare = spare - more
    return np.array(given)


def centred(key, shape, scale, bound, cuts=(), kind=jnp.bfloat16):
    array = jax.random.normal(key, shape, jnp.float32) * scale
    if len(cuts) > 0:
        array = levels(key, shape, cuts, -0.22, 0.18) * array
    return jnp.clip(array, min=-bound, max=bound).astype(kind)


def setup_inputs(seed: int = 0) -> dict:
    seeds = jax.random.split(jax.random.key(seed), 14)
    residual_in = draw_residual_in(jax.random.fold_in(seeds[13], 71), 0)
    ssm_input = centred(seeds[1], (SEQUENCE_TOKENS, MIXER_HEADS * HEAD_DIM), 1.0, 6.0, ((0, 32),))
    ssm_b = centred(seeds[2], (SEQUENCE_TOKENS, STATE), 1.0, 6.0, ((0, 32),))
    ssm_c = centred(seeds[3], (SEQUENCE_TOKENS, STATE), STATE ** -0.5, 0.5, ((0, 32),))
    log_decay = draw_log_decay(jax.random.fold_in(seeds[13], 71), 0)
    skip_gain = jnp.clip(jax.random.uniform(seeds[5], (MIXER_HEADS,), jnp.float32, 0.5, 1.5), 0.5, 1.5)
    out_proj = centred(seeds[6], (MIXER_HEADS * HEAD_DIM, D), (MIXER_HEADS * HEAD_DIM) ** -0.5, 0.125)
    norm_gain = jnp.clip(1.0 + 0.1 * jax.random.normal(seeds[7], (D,), jnp.float32), 0.5, 1.5)
    router = draw_router(jax.random.fold_in(seeds[13], 71), 0)
    assignment_keys = jax.random.split(jax.random.fold_in(seeds[9], 1), SEQUENCE_TOKENS // TOK_DEV)
    assignment_turns = jax.random.permutation(jax.random.fold_in(seeds[9], 3), SEQUENCE_TOKENS // TOK_DEV)
    assignment = jax.vmap(lambda own, number: assign_block(jax.random.fold_in(seeds[9], 2), own, number, TOK_DEV, EXPERTS, 1, CAPACITY, 2))(assignment_keys, assignment_turns).reshape((SEQUENCE_TOKENS, 1))
    expert_gate = centred(seeds[10], (2 * EXPERTS, D, FF // 2), D ** -0.5, 0.125, ((0, 32),))
    expert_up = centred(seeds[11], (2 * EXPERTS, D, FF // 2), D ** -0.5, 0.125, ((0, 32),))
    expert_down = centred(seeds[12], (2 * EXPERTS, FF // 2, D), FF ** -0.5, 0.15625, ((0, 32),))
    return {"residual_in": residual_in, "ssm_input": ssm_input, "ssm_b": ssm_b, "ssm_c": ssm_c, "log_decay": log_decay, "skip_gain": skip_gain, "out_proj": out_proj, "norm_gain": norm_gain, "router": router, "assignment": assignment, "expert_gate": expert_gate, "expert_up": expert_up, "expert_down": expert_down}


def block_terms(values, b_matrix, c_matrix, decay):
    length = values.shape[0]
    values_float = values.astype(jnp.float32)
    cumulative = jnp.cumsum(decay, axis=0)
    weight = jnp.sqrt(-jnp.expm1(2.0 * decay))
    scores = jnp.dot(c_matrix, b_matrix.T, preferred_element_type=jnp.float32)
    leading = cumulative.T
    distance = leading[:, :, None] - leading[:, None, :]
    causal = jnp.arange(length)[:, None] >= jnp.arange(length)[None, :]
    decay_mix = jnp.where(causal[None, :, :], jnp.exp(jnp.minimum(distance, 0.0)), 0.0) * (weight.T[:, None, :] * scores[None, :, :])
    decay_mix = lax.optimization_barrier(decay_mix.astype(jnp.bfloat16))
    inner_part = jnp.einsum('hts,shp->thp', decay_mix.astype(jnp.float32), values_float, precision=lax.Precision.HIGHEST)
    tail_weight = jnp.exp(cumulative[-1][None, :] - cumulative) * weight
    tail_in = lax.optimization_barrier((values_float * tail_weight[:, :, None]).astype(jnp.bfloat16))
    block_state = jnp.einsum('sn,shp->hnp', b_matrix.astype(jnp.float32), tail_in.astype(jnp.float32), precision=lax.Precision.HIGHEST)
    return (inner_part, cumulative, block_state)

def reference(residual_in, ssm_input, ssm_b, ssm_c, log_decay, skip_gain, out_proj, norm_gain, router, assignment, expert_gate, expert_up, expert_down):
    head_count = skip_gain.shape[0]
    total_rows, row_width = ssm_input.shape
    head_size = row_width // head_count
    block_count = total_rows // BLOCK
    values = ssm_input.reshape(block_count, BLOCK, head_count, head_size)
    b_blocks = ssm_b.reshape(block_count, BLOCK, STATE)
    c_blocks = ssm_c.reshape(block_count, BLOCK, STATE)
    d_blocks = log_decay.reshape(block_count, BLOCK, head_count)

    def advance(entry, pieces):
        block_values, b_matrix, c_matrix, decay = pieces
        inner_part, cumulative, block_state = block_terms(block_values, b_matrix, c_matrix, decay)
        entry_rounded = lax.optimization_barrier(entry.astype(jnp.bfloat16))
        carried = jnp.exp(cumulative)[:, :, None] * jnp.einsum('tn,hnp->thp', c_matrix.astype(jnp.float32), entry_rounded.astype(jnp.float32), precision=lax.Precision.HIGHEST)
        updated = jnp.exp(cumulative[-1])[:, None, None] * entry + block_state
        return (updated, inner_part + carried)
    initial = jnp.zeros((head_count, STATE, head_size), jnp.float32)
    final_state, outputs = lax.scan(advance, initial, (values, b_blocks, c_blocks, d_blocks))
    scan_out = (outputs + skip_gain[None, None, :, None] * values.astype(jnp.float32)).reshape(total_rows, row_width).astype(jnp.bfloat16)
    mixed = residual_in.astype(jnp.float32) + jnp.dot(scan_out, out_proj, preferred_element_type=jnp.float32)
    scale = lax.rsqrt(lax.optimization_barrier(jnp.mean(mixed * mixed, axis=1, keepdims=True)) + 1e-05)
    normed = (mixed * scale * norm_gain[None, :]).astype(jnp.bfloat16)
    kernel = jnp.exp(jnp.dot(normed, router, preferred_element_type=jnp.float32))
    column = jnp.ones((EXPERTS,), jnp.float32)
    for sweep in range(SINK_ITERS):
        row_scale = 1.0 / lax.optimization_barrier(jnp.sum(kernel * column[None, :], axis=1))
        column = 1.0 / lax.optimization_barrier(jnp.sum(kernel * row_scale[:, None], axis=0))
    chosen = assignment[:, 0].astype(jnp.int32)
    chosen_hot = chosen[:, None] == jnp.arange(EXPERTS).astype(jnp.int32)[None, :]
    weighted = kernel * column[None, :]
    route_weight = EXPERTS * lax.optimization_barrier(jnp.sum(jnp.where(chosen_hot, weighted, 0.0), axis=1)) / lax.optimization_barrier(jnp.sum(weighted, axis=1))
    device_count = N_SEQ * N_EXP
    hot_int = chosen_hot.astype(jnp.int32).reshape(device_count, TOK_DEV, EXPERTS)
    slot = lax.optimization_barrier(jnp.sum(jnp.cumsum(hot_int, axis=1) * hot_int, axis=2)) - 1
    device_ids = jnp.arange(device_count).astype(jnp.int32)[:, None]
    position = (chosen.reshape(device_count, TOK_DEV) * (device_count * CAPACITY) + device_ids * CAPACITY + slot).reshape(total_rows).astype(jnp.int32)
    buffer = jnp.zeros((EXPERTS * device_count * CAPACITY, D), jnp.bfloat16).at[position].set(normed)
    buffer = buffer.reshape(EXPERTS, device_count * CAPACITY, D)
    gate_pairs = expert_gate.reshape(EXPERTS, 2, D, FF // 2)
    up_pairs = expert_up.reshape(EXPERTS, 2, D, FF // 2)
    down_pairs = expert_down.reshape(EXPERTS, 2, FF // 2, D)

    def run_expert(pieces):
        rows_in, gate_pair, up_pair, down_pair = pieces
        gate_full = jnp.concatenate([gate_pair[0], gate_pair[1]], axis=1)
        up_full = jnp.concatenate([up_pair[0], up_pair[1]], axis=1)
        down_full = jnp.concatenate([down_pair[0], down_pair[1]], axis=0)
        gate_val = jnp.dot(rows_in, gate_full, preferred_element_type=jnp.float32)
        up_val = jnp.dot(rows_in, up_full, preferred_element_type=jnp.float32)
        hidden = (jax.nn.silu(gate_val) * up_val).astype(jnp.bfloat16)
        return jnp.dot(hidden, down_full, preferred_element_type=jnp.float32).astype(jnp.bfloat16)
    results = lax.map(run_expert, (buffer, gate_pairs, up_pairs, down_pairs)).reshape(-1, D)
    expert_out = results[position]
    layer_out = (mixed + route_weight[:, None] * expert_out.astype(jnp.float32)).astype(jnp.bfloat16)
    return (layer_out, route_weight)
```

```python
import functools

import jax
import jax.numpy as jnp
from jax import lax
from jax.experimental import pallas as pl
from jax.experimental.pallas import tpu as pltpu
from jax.sharding import PartitionSpec as P

SINK_ITERS = 8
LANES = 128
TOTAL_ROWS = 16
MESH = pl.DeviceIdType.MESH


def place(flat):
    across = lax.axis_size("exp")
    return (flat // across, flat % across)


def own_index():
    return lax.axis_index("seq") * lax.axis_size("exp") + lax.axis_index("exp")


def device_count():
    return lax.axis_size("seq") * lax.axis_size("exp")


def meet_all(me, devices):
    barrier = pltpu.get_barrier_semaphore()

    @pl.loop(1, devices)
    def _(step):
        pl.semaphore_signal(
            barrier, inc=1, device_id=place((me + step) % devices), device_id_type=MESH
        )

    pl.semaphore_wait(barrier, devices - 1)


def entry_kernel(devices, src_ref, out_ref, arrived, entries, go_send, go_recv, back_send, back_recv, own_sem):
    me = own_index()
    groups = out_ref.shape[1] // LANES
    rows = entries.shape[1]

    def part_of(flat):
        return src_ref.at[flat // groups, :, pl.ds(pl.multiple_of((flat % groups) * LANES, LANES), LANES)]

    def region_of(flat):
        return out_ref.at[
            pl.ds(pl.multiple_of((flat // groups) * rows, rows), rows),
            pl.ds(pl.multiple_of((flat % groups) * LANES, LANES), LANES),
        ]

    def outgoing(peer):
        return pltpu.make_async_remote_copy(
            src_ref=part_of(peer), dst_ref=arrived.at[me], send_sem=go_send.at[peer],
            recv_sem=go_recv.at[me], device_id=place(peer), device_id_type=MESH)

    def incoming(peer):
        return pltpu.make_async_remote_copy(
            src_ref=part_of(peer), dst_ref=arrived.at[peer], send_sem=go_send.at[peer],
            recv_sem=go_recv.at[peer], device_id=place(peer), device_id_type=MESH)

    def returning(peer):
        return pltpu.make_async_remote_copy(
            src_ref=entries.at[peer], dst_ref=region_of(me), send_sem=back_send.at[peer],
            recv_sem=back_recv.at[me], device_id=place(peer), device_id_type=MESH)

    def returned(peer):
        return pltpu.make_async_remote_copy(
            src_ref=entries.at[peer], dst_ref=region_of(peer), send_sem=back_send.at[peer],
            recv_sem=back_recv.at[peer], device_id=place(peer), device_id_type=MESH)

    own = pltpu.make_async_copy(part_of(me), arrived.at[me], own_sem)
    own.start()
    meet_all(me, devices)

    @pl.loop(1, devices)
    def _(step):
        outgoing((me + step) % devices).start()

    own.wait()

    @pl.loop(1, devices)
    def _(step):
        incoming((me + devices - step) % devices).wait_recv()

    def advance(k, state):
        entries[k] = state.astype(entries.dtype)
        block = arrived[k]
        total = jnp.sum(block[rows:rows + TOTAL_ROWS].astype(jnp.float32), axis=0, keepdims=True)
        return jnp.exp(total) * state + block[:rows].astype(jnp.float32)

    lax.fori_loop(0, devices, advance, jnp.zeros((rows, LANES), jnp.float32))

    @pl.loop(1, devices)
    def _(step):
        returning((me + step) % devices).start()

    own_back = pltpu.make_async_copy(entries.at[me], region_of(me), own_sem)
    own_back.start()

    @pl.loop(1, devices)
    def _(step):
        peer = (me + devices - step) % devices
        returned(peer).wait_recv()
        outgoing(peer).wait_send()
        returning(peer).wait_send()

    own_back.wait()


def entering(block_state, total):
    devices = device_count()
    state_size, width = block_state.shape
    parts = devices // (width // LANES)
    rows = state_size // parts
    high = total.astype(jnp.bfloat16)
    low = (total - high.astype(jnp.float32)).astype(jnp.bfloat16)
    totals = jnp.concatenate(
        [high[None], low[None], jnp.zeros((TOTAL_ROWS - 2, width), jnp.bfloat16)], axis=0
    )
    sent = jnp.concatenate(
        [
            block_state.astype(jnp.bfloat16).reshape(parts, rows, width),
            jnp.broadcast_to(totals[None], (parts, TOTAL_ROWS, width)),
        ],
        axis=1,
    )
    dma = pltpu.SemaphoreType.DMA
    return pl.pallas_call(
        functools.partial(entry_kernel, devices),
        out_shape=jax.ShapeDtypeStruct((state_size, width), jnp.bfloat16),
        in_specs=[pl.BlockSpec(memory_space=pltpu.VMEM)],
        out_specs=pl.BlockSpec(memory_space=pltpu.VMEM),
        scratch_shapes=[
            pltpu.VMEM((devices, rows + TOTAL_ROWS, LANES), jnp.bfloat16),
            pltpu.VMEM((devices, rows, LANES), jnp.bfloat16),
            dma((devices,)), dma((devices,)), dma((devices,)), dma((devices,)), dma,
        ],
        compiler_params=pltpu.CompilerParams(collective_id=0, has_side_effects=True),
        name="entry_states",
    )(sent)


def dispatch_kernel(devices, packed_ref, kernel_ref, rows_ref, table_ref,
                    go_send, go_recv, pass_send, pass_recv, table_send, table_recv, own_sem):
    me = own_index()
    side, mine = me % 2, me // 2
    experts = devices // 2
    partner = me + 1 - 2 * side

    def table_copy(peer, slot):
        return pltpu.make_async_remote_copy(
            src_ref=kernel_ref, dst_ref=table_ref.at[slot], send_sem=table_send.at[peer],
            recv_sem=table_recv.at[slot], device_id=place(peer), device_id_type=MESH)

    def row_copy(other, slot):
        return pltpu.make_async_remote_copy(
            src_ref=packed_ref.at[other], dst_ref=rows_ref.at[side, slot], send_sem=go_send.at[other],
            recv_sem=go_recv.at[slot], device_id=place(2 * other + side), device_id_type=MESH)

    def pass_copy(at, slot):
        return pltpu.make_async_remote_copy(
            src_ref=rows_ref.at[side, slot], dst_ref=rows_ref.at[at, slot], send_sem=pass_send.at[slot],
            recv_sem=pass_recv.at[slot], device_id=place(partner), device_id_type=MESH)

    own_rows = pltpu.make_async_copy(packed_ref.at[mine], rows_ref.at[side, mine], own_sem.at[0])
    own_table = pltpu.make_async_copy(kernel_ref, table_ref.at[me], own_sem.at[1])
    own_rows.start()
    own_table.start()
    meet_all(me, devices)

    @pl.loop(1, devices)
    def _(step):
        table_copy((me + step) % devices, me).start()

    @pl.loop(1, experts)
    def _(step):
        row_copy((mine + step) % experts, mine).start()

    own_rows.wait()
    pass_copy(side, mine).start()

    @pl.loop(1, experts)
    def _(step):
        source = (mine + experts - step) % experts
        row_copy(source, source).wait_recv()
        pass_copy(side, source).start()

    own_table.wait()

    @pl.loop(1, devices)
    def _(step):
        peer = (me + devices - step) % devices
        table_copy(peer, peer).wait_recv()
        table_copy(peer, peer).wait_send()

    @pl.loop(0, experts)
    def _(step):
        source = (mine + experts - step) % experts
        pass_copy(1 - side, source).wait_recv()
        pass_copy(side, source).wait_send()

    @pl.loop(1, experts)
    def _(step):
        other = (mine + step) % experts
        row_copy(other, other).wait_send()


def dispatch(packed, kernel):
    devices = device_count()
    experts, capacity, width = packed.shape
    dma = pltpu.SemaphoreType.DMA
    vmem = pl.BlockSpec(memory_space=pltpu.VMEM)
    return pl.pallas_call(
        functools.partial(dispatch_kernel, devices),
        out_shape=(
            jax.ShapeDtypeStruct((2, experts, capacity, width), packed.dtype),
            jax.ShapeDtypeStruct((devices, *kernel.shape), kernel.dtype),
        ),
        in_specs=[vmem, vmem],
        out_specs=(vmem, vmem),
        scratch_shapes=[
            dma((experts,)), dma((experts,)), dma((experts,)), dma((experts,)),
            dma((devices,)), dma((devices,)), dma((2,)),
        ],
        compiler_params=pltpu.CompilerParams(collective_id=1, has_side_effects=True),
        name="dispatch_rows",
    )(packed, kernel)


def collect_kernel(devices, half_ref, out_ref, partial, summed,
                   swap_send, swap_recv, back_send, back_recv, own_sem):
    me = own_index()
    side, mine = me % 2, me // 2
    experts = devices // 2
    partner = me + 1 - 2 * side

    def swap_copy(slot):
        return pltpu.make_async_remote_copy(
            src_ref=half_ref.at[1 - side, slot], dst_ref=partial.at[slot], send_sem=swap_send.at[slot],
            recv_sem=swap_recv.at[slot], device_id=place(partner), device_id_type=MESH)

    def back_copy(other, slot):
        return pltpu.make_async_remote_copy(
            src_ref=summed.at[other], dst_ref=out_ref.at[slot], send_sem=back_send.at[other],
            recv_sem=back_recv.at[slot], device_id=place(2 * other + side), device_id_type=MESH)

    def add_up(slot):
        swap_copy(slot).wait_recv()
        summed[slot] = (
            half_ref[side, slot].astype(jnp.float32) + partial[slot].astype(jnp.float32)
        ).astype(summed.dtype)

    barrier = pltpu.get_barrier_semaphore()

    @pl.loop(1, experts)
    def _(step):
        pl.semaphore_signal(
            barrier, inc=1, device_id=place(2 * ((mine + step) % experts) + side), device_id_type=MESH
        )

    pl.semaphore_signal(barrier, inc=1, device_id=place(partner), device_id_type=MESH)
    pl.semaphore_wait(barrier, experts)

    @pl.loop(1, experts + 1)
    def _(step):
        swap_copy((mine + step) % experts).start()

    @pl.loop(1, experts)
    def _(step):
        other = (mine + step) % experts
        add_up(other)
        back_copy(other, mine).start()

    add_up(mine)
    own = pltpu.make_async_copy(summed.at[mine], out_ref.at[mine], own_sem)
    own.start()

    @pl.loop(1, experts)
    def _(step):
        other = (mine + experts - step) % experts
        back_copy(other, other).wait_recv()
        back_copy(other, other).wait_send()

    @pl.loop(0, experts)
    def _(step):
        swap_copy(step).wait_send()

    own.wait()


def collect(halves):
    devices = device_count()
    _, experts, capacity, width = halves.shape
    dma = pltpu.SemaphoreType.DMA
    vmem = pl.BlockSpec(memory_space=pltpu.VMEM)
    block = pltpu.VMEM((experts, capacity, width), halves.dtype)
    return pl.pallas_call(
        functools.partial(collect_kernel, devices),
        out_shape=jax.ShapeDtypeStruct((experts, capacity, width), halves.dtype),
        in_specs=[vmem],
        out_specs=vmem,
        scratch_shapes=[
            block, block,
            dma((experts,)), dma((experts,)), dma((experts,)), dma((experts,)), dma,
        ],
        compiler_params=pltpu.CompilerParams(collective_id=2, has_side_effects=True),
        name="collect_rows",
    )(halves)


def balance_kernel(table_ref, own_ref, hot_ref, weight_ref):
    devices, experts, length = table_ref.shape
    some = 8

    def sweep(_, column):
        def add(k, totals):
            block = table_ref[pl.ds(pl.multiple_of(k * some, some), some)]
            row_scale = 1.0 / jnp.sum(block * column[None], axis=1, keepdims=True)
            return totals + jnp.sum(block * row_scale, axis=0)

        totals = lax.fori_loop(0, devices // some, add, jnp.zeros((experts, length), jnp.float32))
        return 1.0 / jnp.sum(totals, axis=1, keepdims=True)

    column = lax.fori_loop(0, SINK_ITERS, sweep, jnp.ones((experts, 1), jnp.float32))
    weighted = own_ref[...] * column
    picked = jnp.sum(jnp.where(hot_ref[...] > 0.0, weighted, 0.0), axis=0, keepdims=True)
    weight_ref[...] = experts * picked / jnp.sum(weighted, axis=0, keepdims=True)


def balance(table, own, hot):
    vmem = pl.BlockSpec(memory_space=pltpu.VMEM)
    return pl.pallas_call(
        balance_kernel,
        out_shape=jax.ShapeDtypeStruct((1, own.shape[1]), jnp.float32),
        in_specs=[vmem, vmem, vmem],
        out_specs=vmem,
        name="balance",
    )(table, own, hot)


def widen(per_head, width):
    return jnp.repeat(per_head, width // per_head.shape[-1], axis=-1)


def block_terms(values, b_matrix, c_matrix, decay):
    length, head_count, head_size = values.shape
    row_width = head_count * head_size
    cumulative = jnp.cumsum(decay, axis=0)
    weight = jnp.sqrt(-jnp.expm1(2.0 * decay))
    flat_values = values.reshape(length, row_width)
    tail_weight = jnp.exp(cumulative[-1:] - cumulative) * weight
    tail_in = (flat_values.astype(jnp.float32) * widen(tail_weight, row_width)).astype(jnp.bfloat16)
    block_state = jnp.einsum("sn,sc->nc", b_matrix, tail_in, preferred_element_type=jnp.float32)
    scores = jnp.einsum("tn,sn->ts", c_matrix, b_matrix, preferred_element_type=jnp.float32)
    leading = cumulative.T
    distance = leading[:, :, None] - leading[:, None, :]
    causal = jnp.arange(length)[:, None] >= jnp.arange(length)[None, :]
    decay_mix = jnp.where(causal, jnp.exp(jnp.minimum(distance, 0.0)), 0.0) * (
        weight.T[:, None, :] * scores[None, :, :]
    )
    decay_mix = decay_mix.astype(jnp.bfloat16)
    inner_part = jnp.einsum("hts,shp->thp", decay_mix, values, preferred_element_type=jnp.float32)
    return (inner_part.reshape(length, row_width), cumulative, block_state)


def feed_forward(flat, gate_half, up_half, down_half):
    gate_val = jnp.dot(flat, gate_half, preferred_element_type=jnp.float32)
    up_val = jnp.dot(flat, up_half, preferred_element_type=jnp.float32)
    hidden = (jax.nn.silu(gate_val) * up_val).astype(jnp.bfloat16)
    return jnp.dot(hidden, down_half, preferred_element_type=jnp.float32).astype(jnp.bfloat16)


def per_device(
    residual_in,
    ssm_input,
    ssm_b,
    ssm_c,
    log_decay,
    skip_gain,
    out_proj,
    norm_gain,
    router,
    assignment,
    expert_gate,
    expert_up,
    expert_down,
):
    head_count = skip_gain.shape[0]
    length, row_width = ssm_input.shape
    head_size = row_width // head_count
    model_width = residual_in.shape[1]
    values = ssm_input.reshape(length, head_count, head_size)
    inner_part, cumulative, block_state = block_terms(values, ssm_b, ssm_c, log_decay)
    entry_rounded = entering(block_state, widen(cumulative[-1], row_width))
    carried = widen(jnp.exp(cumulative), row_width) * jnp.dot(
        ssm_c, entry_rounded, preferred_element_type=jnp.float32
    )
    skip_wide = widen(skip_gain, row_width)
    scan_out = (inner_part + carried + skip_wide[None, :] * ssm_input.astype(jnp.float32)).astype(
        jnp.bfloat16
    )
    mixed = residual_in.astype(jnp.float32) + jnp.dot(
        scan_out, out_proj, preferred_element_type=jnp.float32
    )
    scale = lax.rsqrt(jnp.mean(mixed * mixed, axis=1, keepdims=True) + 1e-05)
    normed = (mixed * scale * norm_gain[None, :]).astype(jnp.bfloat16)
    kernel = jnp.exp(jnp.einsum("de,td->et", router, normed, preferred_element_type=jnp.float32))
    experts = router.shape[1]
    capacity = 2 * length // experts
    chosen = assignment[:, 0]
    hot = (chosen[:, None] == jnp.arange(experts, dtype=jnp.int32)[None, :]).astype(jnp.float32)
    upto = (jnp.arange(length)[:, None] >= jnp.arange(length)[None, :]).astype(jnp.bfloat16)
    counts = jnp.dot(upto, hot.astype(jnp.bfloat16), preferred_element_type=jnp.float32)
    slot = jnp.sum(counts * hot, axis=1).astype(jnp.int32) - 1
    position = chosen * capacity + slot
    spread = (
        position[:, None] == jnp.arange(experts * capacity, dtype=jnp.int32)[None, :]
    ).astype(jnp.bfloat16)
    packed = jnp.einsum("ts,td->sd", spread, normed, preferred_element_type=jnp.float32)
    packed = packed.astype(jnp.bfloat16).reshape(experts, capacity, model_width)
    arrived, table = dispatch(packed, kernel)
    route_weight = balance(table, kernel, hot.T)[0]
    halves = feed_forward(
        arrived.reshape(2 * experts * capacity, model_width),
        expert_gate[0],
        expert_up[0],
        expert_down[0],
    )
    summed = collect(halves.reshape(2, experts, capacity, model_width))
    expert_out = jnp.dot(
        spread, summed.reshape(experts * capacity, model_width), preferred_element_type=jnp.float32
    )
    layer_out = (mixed + route_weight[:, None] * expert_out).astype(jnp.bfloat16)
    return (layer_out, route_weight)


def solution(mesh):
    in_specs = (
        P(("seq", "exp"), None),
        P(("seq", "exp"), None),
        P(("seq", "exp"), None),
        P(("seq", "exp"), None),
        P(("seq", "exp"), None),
        P(),
        P(),
        P(),
        P(),
        P(("seq", "exp"), None),
        P(("seq", "exp"), None, None),
        P(("seq", "exp"), None, None),
        P(("seq", "exp"), None, None),
    )
    out_specs = (P(("seq", "exp"), None), P(("seq", "exp")))
    return jax.shard_map(
        per_device, mesh=mesh, in_specs=in_specs, out_specs=out_specs, check_vma=False
    )
```

```python
import functools

import jax
import jax.numpy as jnp
from jax import lax
from jax.experimental import pallas as pl
from jax.experimental.pallas import tpu as pltpu
from jax.sharding import PartitionSpec as P

SINK_ITERS = 8
LANES = 128
TOTAL_ROWS = 16
MESH = pl.DeviceIdType.MESH


def place(flat):
    across = lax.axis_size("exp")
    return (flat // across, flat % across)


def own_index():
    return lax.axis_index("seq") * lax.axis_size("exp") + lax.axis_index("exp")


def device_count():
    return lax.axis_size("seq") * lax.axis_size("exp")


def meet_all(me, devices):
    barrier = pltpu.get_barrier_semaphore()

    @pl.loop(1, devices)
    def _(step):
        pl.semaphore_signal(
            barrier, inc=1, device_id=place((me + step) % devices), device_id_type=MESH
        )

    pl.semaphore_wait(barrier, devices - 1)


def entry_kernel(devices, src_ref, out_ref, arrived, entries, go_send, go_recv, back_send, back_recv, own_sem):
    me = own_index()
    groups = out_ref.shape[1] // LANES
    rows = entries.shape[1]

    def part_of(flat):
        return src_ref.at[flat // groups, :, pl.ds(pl.multiple_of((flat % groups) * LANES, LANES), LANES)]

    def region_of(flat):
        return out_ref.at[
            pl.ds(pl.multiple_of((flat // groups) * rows, rows), rows),
            pl.ds(pl.multiple_of((flat % groups) * LANES, LANES), LANES),
        ]

    def outgoing(peer):
        return pltpu.make_async_remote_copy(
            src_ref=part_of(peer), dst_ref=arrived.at[me], send_sem=go_send.at[peer],
            recv_sem=go_recv.at[me], device_id=place(peer), device_id_type=MESH)

    def incoming(peer):
        return pltpu.make_async_remote_copy(
            src_ref=part_of(peer), dst_ref=arrived.at[peer], send_sem=go_send.at[peer],
            recv_sem=go_recv.at[peer], device_id=place(peer), device_id_type=MESH)

    def returning(peer):
        return pltpu.make_async_remote_copy(
            src_ref=entries.at[peer], dst_ref=region_of(me), send_sem=back_send.at[peer],
            recv_sem=back_recv.at[me], device_id=place(peer), device_id_type=MESH)

    def returned(peer):
        return pltpu.make_async_remote_copy(
            src_ref=entries.at[peer], dst_ref=region_of(peer), send_sem=back_send.at[peer],
            recv_sem=back_recv.at[peer], device_id=place(peer), device_id_type=MESH)

    own = pltpu.make_async_copy(part_of(me), arrived.at[me], own_sem)
    own.start()
    meet_all(me, devices)

    @pl.loop(1, devices)
    def _(step):
        outgoing((me + step) % devices).start()

    own.wait()

    @pl.loop(1, devices)
    def _(step):
        incoming((me + devices - step) % devices).wait_recv()

    def advance(k, state):
        entries[k] = state.astype(entries.dtype)
        block = arrived[k]
        total = jnp.sum(block[rows:rows + TOTAL_ROWS].astype(jnp.float32), axis=0, keepdims=True)
        return jnp.exp(total) * state + block[:rows].astype(jnp.float32)

    lax.fori_loop(0, devices, advance, jnp.zeros((rows, LANES), jnp.float32))

    @pl.loop(1, devices)
    def _(step):
        returning((me + step) % devices).start()

    own_back = pltpu.make_async_copy(entries.at[me], region_of(me), own_sem)
    own_back.start()

    @pl.loop(1, devices)
    def _(step):
        peer = (me + devices - step) % devices
        returned(peer).wait_recv()
        outgoing(peer).wait_send()
        returning(peer).wait_send()

    own_back.wait()


def entering(block_state, total):
    devices = device_count()
    state_size, width = block_state.shape
    parts = devices // (width // LANES)
    rows = state_size // parts
    high = total.astype(jnp.bfloat16)
    low = (total - high.astype(jnp.float32)).astype(jnp.bfloat16)
    totals = jnp.concatenate(
        [high[None], low[None], jnp.zeros((TOTAL_ROWS - 2, width), jnp.bfloat16)], axis=0
    )
    sent = jnp.concatenate(
        [
            block_state.astype(jnp.bfloat16).reshape(parts, rows, width),
            jnp.broadcast_to(totals[None], (parts, TOTAL_ROWS, width)),
        ],
        axis=1,
    )
    dma = pltpu.SemaphoreType.DMA
    return pl.pallas_call(
        functools.partial(entry_kernel, devices),
        out_shape=jax.ShapeDtypeStruct((state_size, width), jnp.bfloat16),
        in_specs=[pl.BlockSpec(memory_space=pltpu.VMEM)],
        out_specs=pl.BlockSpec(memory_space=pltpu.VMEM),
        scratch_shapes=[
            pltpu.VMEM((devices, rows + TOTAL_ROWS, LANES), jnp.bfloat16),
            pltpu.VMEM((devices, rows, LANES), jnp.bfloat16),
            dma((devices,)), dma((devices,)), dma((devices,)), dma((devices,)), dma,
        ],
        compiler_params=pltpu.CompilerParams(collective_id=0, has_side_effects=True),
        name="entry_states",
    )(sent)


def expert_kernel(devices, group, packed_ref, kernel_ref, gate_hbm, up_hbm, down_hbm, out_ref, table_ref,
                  rows, halves, partial, summed, gate, up, down, block,
                  go_send, go_recv, pass_send, pass_recv, swap_send, swap_recv, back_send, back_recv,
                  near_send, near_recv, far_send, far_recv, own_sem, weight_sem):
    line, spot = lax.axis_index("seq"), lax.axis_index("exp")
    lines, spots = lax.axis_size("seq"), lax.axis_size("exp")
    me = line * spots + spot
    side, mine = me % 2, me // 2
    experts = devices // 2
    partner = me + 1 - 2 * side
    capacity, width = packed_ref.shape[1:]
    turns = experts // group

    def remote(src, dst, send, recv, device):
        return pltpu.make_async_remote_copy(
            src_ref=src, dst_ref=dst, send_sem=send, recv_sem=recv, device_id=device, device_id_type=MESH)

    def row_copy(other, slot):
        return remote(packed_ref.at[other], rows.at[side, slot], go_send.at[other], go_recv.at[slot],
                      place(2 * other + side))

    def pass_copy(at, slot):
        return remote(rows.at[side, slot], rows.at[at, slot], pass_send.at[slot], pass_recv.at[slot],
                      place(partner))

    def swap_copy(slot):
        return remote(halves.at[1 - side, slot], partial.at[slot], swap_send.at[slot], swap_recv.at[slot],
                      place(partner))

    def back_copy(other, slot):
        return remote(summed.at[other], out_ref.at[slot], back_send.at[other], back_recv.at[slot],
                      place(2 * other + side))

    def near_copy(other, slot):
        return remote(kernel_ref, table_ref.at[line, slot], near_send.at[other], near_recv.at[slot],
                      (line, other))

    def far_copy(other, slot):
        return remote(table_ref.at[line], table_ref.at[slot], far_send.at[other], far_recv.at[slot],
                      (other, spot))

    own_rows = pltpu.make_async_copy(packed_ref.at[mine], rows.at[side, mine], own_sem.at[0])
    own_table = pltpu.make_async_copy(kernel_ref, table_ref.at[line, spot], own_sem.at[1])
    own_rows.start()
    own_table.start()
    loads = [
        pltpu.make_async_copy(gate_hbm, gate, weight_sem.at[0]),
        pltpu.make_async_copy(up_hbm, up, weight_sem.at[1]),
        pltpu.make_async_copy(down_hbm, down, weight_sem.at[2]),
    ]
    for load in loads:
        load.start()
    meet_all(me, devices)

    @pl.loop(1, experts)
    def _(step):
        row_copy((mine + step) % experts, mine).start()

    @pl.loop(1, spots)
    def _(step):
        near_copy((spot + step) % spots, spot).start()

    own_rows.wait()
    pass_copy(side, mine).start()
    for load in loads:
        load.wait()

    def source_of(turn, at):
        return (mine + 2 * experts - (turn * group + at)) % experts

    @pl.loop(0, turns + 2)
    def _(turn):
        @pl.when(turn < turns)
        def _():
            @pl.loop(0, group)
            def _(at):
                @pl.when(turn * group + at > 0)
                def _():
                    source = source_of(turn, at)
                    row_copy(source, source).wait_recv()
                    pass_copy(side, source).start()

        @pl.when((turn >= 1) & (turn <= turns))
        def _():
            @pl.loop(0, group)
            def _(at):
                pass_copy(1 - side, source_of(turn - 1, at)).wait_recv()

            sources = [source_of(turn - 1, at) for at in range(group)]
            places = [(k, source, (k * group + at) * capacity)
                      for k in range(2) for at, source in enumerate(sources)]
            for k, source, start in places:
                block[start:start + capacity] = rows[k, source]
            taken = block[...]
            across = (((1,), (1,)), ((), ()))
            gate_val = lax.dot_general(taken, gate[...], across, preferred_element_type=jnp.float32)
            up_val = lax.dot_general(taken, up[...], across, preferred_element_type=jnp.float32)
            hidden = (gate_val / (1.0 + jnp.exp(-gate_val)) * up_val).astype(jnp.bfloat16)
            piece = 512
            for column in range(0, width, piece):
                made = jnp.dot(hidden, down[:, column:column + piece], preferred_element_type=jnp.float32)
                made = made.astype(halves.dtype)
                for k, source, start in places:
                    halves[k, source, :, column:column + piece] = made[start:start + capacity]

            @pl.loop(0, group)
            def _(at):
                swap_copy(source_of(turn - 1, at)).start()

        @pl.when(turn >= 2)
        def _():
            @pl.loop(0, group)
            def _(at):
                source = source_of(turn - 2, at)
                swap_copy(source).wait_recv()
                summed[source] = (
                    halves[side, source].astype(jnp.float32) + partial[source].astype(jnp.float32)
                ).astype(summed.dtype)

                @pl.when((turn - 2) * group + at > 0)
                def _():
                    back_copy(source, mine).start()

        @pl.when(turn == 1)
        def _():
            own_table.wait()

            @pl.loop(1, spots)
            def _(step):
                near_copy((spot + step) % spots, (spot + step) % spots).wait_recv()

            @pl.loop(1, lines)
            def _(step):
                far_copy((line + step) % lines, line).start()

    own_out = pltpu.make_async_copy(summed.at[mine], out_ref.at[mine], own_sem.at[0])
    own_out.start()

    @pl.loop(1, lines)
    def _(step):
        other = (line + step) % lines
        far_copy(other, other).wait_recv()
        far_copy(other, other).wait_send()

    @pl.loop(1, spots)
    def _(step):
        near_copy((spot + step) % spots, spot).wait_send()

    @pl.loop(0, experts)
    def _(step):
        pass_copy(side, step).wait_send()
        swap_copy(step).wait_send()

    @pl.loop(1, experts)
    def _(step):
        other = (mine + step) % experts
        row_copy(other, other).wait_send()
        back_copy(other, other).wait_recv()
        back_copy(other, other).wait_send()

    own_out.wait()


def expert_layer(packed, kernel, gate_half, up_half, down_half):
    devices = device_count()
    lines, spots = lax.axis_size("seq"), lax.axis_size("exp")
    experts, capacity, width = packed.shape
    hidden_units = down_half.shape[0]
    group = 4
    dma = pltpu.SemaphoreType.DMA
    vmem = pl.BlockSpec(memory_space=pltpu.VMEM)
    anywhere = pl.BlockSpec(memory_space=pl.ANY)
    single = pltpu.VMEM((experts, capacity, width), packed.dtype)
    double = pltpu.VMEM((2, experts, capacity, width), packed.dtype)
    weights = pltpu.VMEM((hidden_units, width), packed.dtype)
    each = dma((experts,))
    return pl.pallas_call(
        functools.partial(expert_kernel, devices, group),
        out_shape=(
            jax.ShapeDtypeStruct((experts, capacity, width), packed.dtype),
            jax.ShapeDtypeStruct((lines, spots, *kernel.shape), kernel.dtype),
        ),
        in_specs=[vmem, vmem, anywhere, anywhere, anywhere],
        out_specs=(vmem, vmem),
        scratch_shapes=[
            double, double, single, single, weights, weights, weights,
            pltpu.VMEM((2 * group * capacity, width), packed.dtype),
            each, each, each, each, each, each, each, each,
            dma((spots,)), dma((spots,)), dma((lines,)), dma((lines,)), dma((2,)), dma((3,)),
        ],
        compiler_params=pltpu.CompilerParams(collective_id=1, has_side_effects=True),
        name="expert_layer",
    )(packed, kernel, gate_half.T, up_half.T, down_half)


def balance_kernel(table_ref, own_ref, hot_ref, weight_ref):
    devices, experts, length = table_ref.shape
    some = 8

    def sweep(_, column):
        def add(k, totals):
            block = table_ref[pl.ds(pl.multiple_of(k * some, some), some)]
            row_scale = 1.0 / jnp.sum(block * column[None], axis=1, keepdims=True)
            return totals + jnp.sum(block * row_scale, axis=0)

        totals = lax.fori_loop(0, devices // some, add, jnp.zeros((experts, length), jnp.float32))
        return 1.0 / jnp.sum(totals, axis=1, keepdims=True)

    column = lax.fori_loop(0, SINK_ITERS, sweep, jnp.ones((experts, 1), jnp.float32))
    weighted = own_ref[...] * column
    picked = jnp.sum(jnp.where(hot_ref[...] > 0.0, weighted, 0.0), axis=0, keepdims=True)
    weight_ref[...] = experts * picked / jnp.sum(weighted, axis=0, keepdims=True)


def balance(table, own, hot):
    vmem = pl.BlockSpec(memory_space=pltpu.VMEM)
    return pl.pallas_call(
        balance_kernel,
        out_shape=jax.ShapeDtypeStruct((1, own.shape[1]), jnp.float32),
        in_specs=[vmem, vmem, vmem],
        out_specs=vmem,
        name="balance",
    )(table, own, hot)


def widen(per_head, width):
    return jnp.repeat(per_head, width // per_head.shape[-1], axis=-1)


def block_terms(values, b_matrix, c_matrix, decay):
    length, head_count, head_size = values.shape
    row_width = head_count * head_size
    cumulative = jnp.cumsum(decay, axis=0)
    weight = jnp.sqrt(-jnp.expm1(2.0 * decay))
    flat_values = values.reshape(length, row_width)
    tail_weight = jnp.exp(cumulative[-1:] - cumulative) * weight
    tail_in = (flat_values.astype(jnp.float32) * widen(tail_weight, row_width)).astype(jnp.bfloat16)
    block_state = jnp.einsum("sn,sc->nc", b_matrix, tail_in, preferred_element_type=jnp.float32)
    scores = jnp.einsum("tn,sn->ts", c_matrix, b_matrix, preferred_element_type=jnp.float32)
    leading = cumulative.T
    distance = leading[:, :, None] - leading[:, None, :]
    causal = jnp.arange(length)[:, None] >= jnp.arange(length)[None, :]
    decay_mix = jnp.where(causal, jnp.exp(jnp.minimum(distance, 0.0)), 0.0) * (
        weight.T[:, None, :] * scores[None, :, :]
    )
    decay_mix = decay_mix.astype(jnp.bfloat16)
    inner_part = jnp.einsum("hts,shp->thp", decay_mix, values, preferred_element_type=jnp.float32)
    return (inner_part.reshape(length, row_width), cumulative, block_state)


def per_device(
    residual_in,
    ssm_input,
    ssm_b,
    ssm_c,
    log_decay,
    skip_gain,
    out_proj,
    norm_gain,
    router,
    assignment,
    expert_gate,
    expert_up,
    expert_down,
):
    head_count = skip_gain.shape[0]
    length, row_width = ssm_input.shape
    head_size = row_width // head_count
    model_width = residual_in.shape[1]
    values = ssm_input.reshape(length, head_count, head_size)
    inner_part, cumulative, block_state = block_terms(values, ssm_b, ssm_c, log_decay)
    entry_rounded = entering(block_state, widen(cumulative[-1], row_width))
    carried = widen(jnp.exp(cumulative), row_width) * jnp.dot(
        ssm_c, entry_rounded, preferred_element_type=jnp.float32
    )
    skip_wide = widen(skip_gain, row_width)
    scan_out = (inner_part + carried + skip_wide[None, :] * ssm_input.astype(jnp.float32)).astype(
        jnp.bfloat16
    )
    mixed = residual_in.astype(jnp.float32) + jnp.dot(
        scan_out, out_proj, preferred_element_type=jnp.float32
    )
    scale = lax.rsqrt(jnp.mean(mixed * mixed, axis=1, keepdims=True) + 1e-05)
    normed = (mixed * scale * norm_gain[None, :]).astype(jnp.bfloat16)
    kernel = jnp.exp(jnp.einsum("de,td->et", router, normed, preferred_element_type=jnp.float32))
    experts = router.shape[1]
    capacity = max(16, 2 * length // experts)
    chosen = assignment[:, 0]
    hot = (chosen[:, None] == jnp.arange(experts, dtype=jnp.int32)[None, :]).astype(jnp.float32)
    upto = (jnp.arange(length)[:, None] >= jnp.arange(length)[None, :]).astype(jnp.bfloat16)
    counts = jnp.dot(upto, hot.astype(jnp.bfloat16), preferred_element_type=jnp.float32)
    slot = jnp.sum(counts * hot, axis=1).astype(jnp.int32) - 1
    position = chosen * capacity + slot
    spread = (
        position[:, None] == jnp.arange(experts * capacity, dtype=jnp.int32)[None, :]
    ).astype(jnp.bfloat16)
    packed = jnp.einsum("ts,td->sd", spread, normed, preferred_element_type=jnp.float32)
    packed = packed.astype(jnp.bfloat16).reshape(experts, capacity, model_width)
    summed, table = expert_layer(packed, kernel, expert_gate[0], expert_up[0], expert_down[0])
    route_weight = balance(table.reshape(-1, experts, length), kernel, hot.T)[0]
    expert_out = jnp.dot(
        spread, summed.reshape(experts * capacity, model_width), preferred_element_type=jnp.float32
    )
    layer_out = (mixed + route_weight[:, None] * expert_out).astype(jnp.bfloat16)
    return (layer_out, route_weight)


def solution(mesh):
    in_specs = (
        P(("seq", "exp"), None),
        P(("seq", "exp"), None),
        P(("seq", "exp"), None),
        P(("seq", "exp"), None),
        P(("seq", "exp"), None),
        P(),
        P(),
        P(),
        P(),
        P(("seq", "exp"), None),
        P(("seq", "exp"), None, None),
        P(("seq", "exp"), None, None),
        P(("seq", "exp"), None, None),
    )
    out_specs = (P(("seq", "exp"), None), P(("seq", "exp")))
    return jax.shard_map(
        per_device, mesh=mesh, in_specs=in_specs, out_specs=out_specs, check_vma=False
    )
```

```python
import functools

import jax
import jax.numpy as jnp
from jax import lax
from jax.experimental import pallas as pl
from jax.experimental.pallas import tpu as pltpu
from jax.sharding import PartitionSpec as P

SINK_ITERS = 8
LANES = 128
MESH = pl.DeviceIdType.MESH


def place(flat):
    across = lax.axis_size("exp")
    return (flat // across, flat % across)


def own_index():
    return lax.axis_index("seq") * lax.axis_size("exp") + lax.axis_index("exp")


def device_count():
    return lax.axis_size("seq") * lax.axis_size("exp")


def meet_all(me, devices):
    barrier = pltpu.get_barrier_semaphore()

    @pl.loop(1, devices)
    def _(step):
        pl.semaphore_signal(
            barrier, inc=1, device_id=place((me + step) % devices), device_id_type=MESH
        )

    pl.semaphore_wait(barrier, devices - 1)


def entry_kernel(devices, pieces, src_ref, factor_ref, out_ref, arrived, entries, factors,
                 go_send, go_recv, factor_send, factor_recv, back_send, back_recv, own_sem):
    me = own_index()
    groups = out_ref.shape[1] // LANES
    rows = arrived.shape[2]

    def region(ref, flat, piece):
        return ref.at[
            pl.ds(pl.multiple_of(((flat // groups) * pieces + piece) * rows, rows), rows),
            pl.ds(pl.multiple_of((flat % groups) * LANES, LANES), LANES),
        ]

    def remote(src, dst, send, recv, peer):
        return pltpu.make_async_remote_copy(
            src_ref=src, dst_ref=dst, send_sem=send, recv_sem=recv, device_id=place(peer), device_id_type=MESH)

    def state_copy(piece, peer, slot):
        return remote(region(src_ref, peer, piece), arrived.at[piece, slot], go_send.at[piece, peer],
                      go_recv.at[piece, slot], peer)

    def factor_copy(peer, slot):
        return remote(factor_ref.at[peer % groups], factors.at[slot], factor_send.at[peer],
                      factor_recv.at[slot], peer)

    def entry_copy(piece, peer, slot):
        return remote(entries.at[piece, peer], region(out_ref, slot, piece), back_send.at[piece, peer],
                      back_recv.at[piece, slot], peer)

    own_factor = pltpu.make_async_copy(factor_ref.at[me % groups], factors.at[me], own_sem.at[0])
    own_state = [
        pltpu.make_async_copy(region(src_ref, me, piece), arrived.at[piece, me], own_sem.at[1 + piece])
        for piece in range(pieces)
    ]
    own_factor.start()
    for piece in range(pieces):
        own_state[piece].start()
    meet_all(me, devices)

    @pl.loop(1, devices)
    def _(step):
        peer = (me + step) % devices
        factor_copy(peer, me).start()
        state_copy(0, peer, me).start()

    for piece in range(1, pieces):
        @pl.loop(1, devices)
        def _(step):
            state_copy(piece, (me + step) % devices, me).start()

    own_factor.wait()
    for piece in range(pieces):
        own_state[piece].wait()

        @pl.loop(1, devices)
        def _(step):
            peer = (me + devices - step) % devices
            if piece == 0:
                factor_copy(peer, peer).wait_recv()
            state_copy(piece, peer, peer).wait_recv()

        def advance(k, state):
            entries[piece, k] = state.astype(entries.dtype)
            return factors[k] * state + arrived[piece, k].astype(jnp.float32)

        lax.fori_loop(0, devices, advance, jnp.zeros((rows, LANES), jnp.float32))

        @pl.loop(1, devices)
        def _(step):
            entry_copy(piece, (me + step) % devices, me).start()

    own_back = [
        pltpu.make_async_copy(entries.at[piece, me], region(out_ref, me, piece), own_sem.at[1 + piece])
        for piece in range(pieces)
    ]
    for piece in range(pieces):
        own_back[piece].start()

    @pl.loop(1, devices)
    def _(step):
        peer = (me + devices - step) % devices
        factor_copy(peer, peer).wait_send()
        for piece in range(pieces):
            state_copy(piece, peer, peer).wait_send()
            entry_copy(piece, peer, peer).wait_recv()
            entry_copy(piece, peer, peer).wait_send()

    for piece in range(pieces):
        own_back[piece].wait()


def entering(block_state, factor):
    devices = device_count()
    state_size, width = block_state.shape
    groups = width // LANES
    rows = state_size * groups // devices
    pieces = 2 if rows % 32 == 0 else 1
    dma = pltpu.SemaphoreType.DMA
    vmem = pl.BlockSpec(memory_space=pltpu.VMEM)
    held = pltpu.VMEM((pieces, devices, rows // pieces, LANES), jnp.bfloat16)
    each = dma((pieces, devices))
    return pl.pallas_call(
        functools.partial(entry_kernel, devices, pieces),
        out_shape=jax.ShapeDtypeStruct((state_size, width), jnp.bfloat16),
        in_specs=[vmem, vmem],
        out_specs=vmem,
        scratch_shapes=[
            held, held, pltpu.VMEM((devices, 1, LANES), jnp.float32),
            each, each, dma((devices,)), dma((devices,)), each, each, dma((1 + pieces,)),
        ],
        compiler_params=pltpu.CompilerParams(collective_id=0, has_side_effects=True),
        name="entry_states",
    )(block_state.astype(jnp.bfloat16), factor.reshape(groups, 1, LANES))


def expert_kernel(devices, group, packed_ref, kernel_ref, hot_ref, gate_hbm, up_hbm, down_hbm, out_ref, weight_ref,
                  table_ref, rows, halves, partial, summed, gate, up, down, block,
                  go_send, go_recv, pass_send, pass_recv, swap_send, swap_recv, back_send, back_recv,
                  near_send, near_recv, far_send, far_recv, own_sem, weight_sem):
    line, spot = lax.axis_index("seq"), lax.axis_index("exp")
    lines, spots = lax.axis_size("seq"), lax.axis_size("exp")
    me = line * spots + spot
    side, mine = me % 2, me // 2
    experts = devices // 2
    partner = me + 1 - 2 * side
    capacity, width = packed_ref.shape[1:]
    turns = experts // group

    def remote(src, dst, send, recv, device):
        return pltpu.make_async_remote_copy(
            src_ref=src, dst_ref=dst, send_sem=send, recv_sem=recv, device_id=device, device_id_type=MESH)

    def row_copy(other, slot):
        return remote(packed_ref.at[other], rows.at[side, slot], go_send.at[other], go_recv.at[slot],
                      place(2 * other + side))

    def pass_copy(at, slot):
        return remote(rows.at[side, slot], rows.at[at, slot], pass_send.at[slot], pass_recv.at[slot],
                      place(partner))

    def swap_copy(slot):
        return remote(halves.at[1 - side, slot], partial.at[slot], swap_send.at[slot], swap_recv.at[slot],
                      place(partner))

    def back_copy(other, slot):
        return remote(summed.at[other], out_ref.at[slot], back_send.at[other], back_recv.at[slot],
                      place(2 * other + side))

    def near_copy(other, slot):
        return remote(kernel_ref, table_ref.at[line, slot], near_send.at[other], near_recv.at[slot],
                      (line, other))

    def far_copy(other, slot):
        return remote(table_ref.at[line], table_ref.at[slot], far_send.at[other], far_recv.at[slot],
                      (other, spot))

    own_rows = pltpu.make_async_copy(packed_ref.at[mine], rows.at[side, mine], own_sem.at[0])
    own_table = pltpu.make_async_copy(kernel_ref, table_ref.at[line, spot], own_sem.at[1])
    own_rows.start()
    own_table.start()
    loads = [
        pltpu.make_async_copy(gate_hbm, gate, weight_sem.at[0]),
        pltpu.make_async_copy(up_hbm, up, weight_sem.at[1]),
        pltpu.make_async_copy(down_hbm, down, weight_sem.at[2]),
    ]
    for load in loads:
        load.start()
    meet_all(me, devices)

    @pl.loop(1, experts)
    def _(step):
        row_copy((mine + step) % experts, mine).start()

    @pl.loop(1, spots)
    def _(step):
        near_copy((spot + step) % spots, spot).start()

    own_rows.wait()
    pass_copy(side, mine).start()
    for load in loads:
        load.wait()

    def source_of(turn, at):
        return (mine + 2 * experts - (turn * group + at)) % experts

    @pl.loop(0, turns + 2)
    def _(turn):
        @pl.when(turn < turns)
        def _():
            @pl.loop(0, group)
            def _(at):
                @pl.when(turn * group + at > 0)
                def _():
                    source = source_of(turn, at)
                    row_copy(source, source).wait_recv()
                    pass_copy(side, source).start()

        @pl.when((turn >= 1) & (turn <= turns))
        def _():
            @pl.loop(0, group)
            def _(at):
                pass_copy(1 - side, source_of(turn - 1, at)).wait_recv()

            sources = [source_of(turn - 1, at) for at in range(group)]
            places = [(k, source, (k * group + at) * capacity)
                      for k in range(2) for at, source in enumerate(sources)]
            for k, source, start in places:
                block[start:start + capacity] = rows[k, source]
            taken = block[...]
            across = (((1,), (1,)), ((), ()))
            gate_val = lax.dot_general(taken, gate[...], across, preferred_element_type=jnp.float32)
            up_val = lax.dot_general(taken, up[...], across, preferred_element_type=jnp.float32)
            hidden = (gate_val / (1.0 + jnp.exp(-gate_val)) * up_val).astype(jnp.bfloat16)
            piece = 512
            for column in range(0, width, piece):
                made = jnp.dot(hidden, down[:, column:column + piece], preferred_element_type=jnp.float32)
                made = made.astype(halves.dtype)
                for k, source, start in places:
                    halves[k, source, :, column:column + piece] = made[start:start + capacity]

            @pl.loop(0, group)
            def _(at):
                swap_copy(source_of(turn - 1, at)).start()

        @pl.when(turn >= 2)
        def _():
            @pl.loop(0, group)
            def _(at):
                source = source_of(turn - 2, at)
                swap_copy(source).wait_recv()
                summed[source] = (
                    halves[side, source].astype(jnp.float32) + partial[source].astype(jnp.float32)
                ).astype(summed.dtype)

                @pl.when((turn - 2) * group + at > 0)
                def _():
                    back_copy(source, mine).start()

        @pl.when(turn == 1)
        def _():
            own_table.wait()

            @pl.loop(1, spots)
            def _(step):
                near_copy((spot + step) % spots, (spot + step) % spots).wait_recv()

            @pl.loop(1, lines)
            def _(step):
                far_copy((line + step) % lines, line).start()

    own_out = pltpu.make_async_copy(summed.at[mine], out_ref.at[mine], own_sem.at[0])
    own_out.start()

    @pl.loop(1, lines)
    def _(step):
        other = (line + step) % lines
        far_copy(other, other).wait_recv()
        far_copy(other, other).wait_send()

    choices, length = kernel_ref.shape

    def sweep(_, column):
        def add(at, totals):
            part = table_ref[at]
            row_scale = 1.0 / jnp.sum(part * column[None], axis=1, keepdims=True)
            return totals + jnp.sum(part * row_scale, axis=0)

        totals = lax.fori_loop(0, lines, add, jnp.zeros((choices, length), jnp.float32))
        return 1.0 / jnp.sum(totals, axis=1, keepdims=True)

    column = lax.fori_loop(0, SINK_ITERS, sweep, jnp.ones((choices, 1), jnp.float32))
    weighted = kernel_ref[...] * column
    picked = jnp.sum(jnp.where(hot_ref[...] > 0.0, weighted, 0.0), axis=0, keepdims=True)
    weight_ref[...] = choices * picked / jnp.sum(weighted, axis=0, keepdims=True)

    @pl.loop(1, spots)
    def _(step):
        near_copy((spot + step) % spots, spot).wait_send()

    @pl.loop(0, experts)
    def _(step):
        pass_copy(side, step).wait_send()
        swap_copy(step).wait_send()

    @pl.loop(1, experts)
    def _(step):
        other = (mine + step) % experts
        row_copy(other, other).wait_send()
        back_copy(other, other).wait_recv()
        back_copy(other, other).wait_send()

    own_out.wait()


def expert_layer(packed, kernel, hot, gate_half, up_half, down_half):
    devices = device_count()
    lines, spots = lax.axis_size("seq"), lax.axis_size("exp")
    experts, capacity, width = packed.shape
    hidden_units = down_half.shape[0]
    group = 4
    dma = pltpu.SemaphoreType.DMA
    vmem = pl.BlockSpec(memory_space=pltpu.VMEM)
    anywhere = pl.BlockSpec(memory_space=pl.ANY)
    single = pltpu.VMEM((experts, capacity, width), packed.dtype)
    double = pltpu.VMEM((2, experts, capacity, width), packed.dtype)
    weights = pltpu.VMEM((hidden_units, width), packed.dtype)
    each = dma((experts,))
    return pl.pallas_call(
        functools.partial(expert_kernel, devices, group),
        out_shape=(
            jax.ShapeDtypeStruct((experts, capacity, width), packed.dtype),
            jax.ShapeDtypeStruct((1, kernel.shape[1]), kernel.dtype),
        ),
        in_specs=[vmem, vmem, vmem, anywhere, anywhere, anywhere],
        out_specs=(vmem, vmem),
        scratch_shapes=[
            pltpu.VMEM((lines, spots, *kernel.shape), kernel.dtype),
            double, double, single, single, weights, weights, weights,
            pltpu.VMEM((2 * group * capacity, width), packed.dtype),
            each, each, each, each, each, each, each, each,
            dma((spots,)), dma((spots,)), dma((lines,)), dma((lines,)), dma((2,)), dma((3,)),
        ],
        compiler_params=pltpu.CompilerParams(collective_id=1, has_side_effects=True),
        name="expert_layer",
    )(packed, kernel, hot, gate_half.T, up_half.T, down_half)


def widen(per_head, width):
    return jnp.repeat(per_head, width // per_head.shape[-1], axis=-1)


def block_terms(values, b_matrix, c_matrix, decay):
    length, head_count, head_size = values.shape
    row_width = head_count * head_size
    cumulative = jnp.cumsum(decay, axis=0)
    weight = jnp.sqrt(-jnp.expm1(2.0 * decay))
    flat_values = values.reshape(length, row_width)
    tail_weight = jnp.exp(cumulative[-1:] - cumulative) * weight
    tail_in = (flat_values.astype(jnp.float32) * widen(tail_weight, row_width)).astype(jnp.bfloat16)
    block_state = jnp.einsum("sn,sc->nc", b_matrix, tail_in, preferred_element_type=jnp.float32)
    scores = jnp.einsum("tn,sn->ts", c_matrix, b_matrix, preferred_element_type=jnp.float32)
    leading = cumulative.T
    distance = leading[:, :, None] - leading[:, None, :]
    causal = jnp.arange(length)[:, None] >= jnp.arange(length)[None, :]
    decay_mix = jnp.where(causal, jnp.exp(jnp.minimum(distance, 0.0)), 0.0) * (
        weight.T[:, None, :] * scores[None, :, :]
    )
    decay_mix = decay_mix.astype(jnp.bfloat16)
    inner_part = jnp.einsum("hts,shp->thp", decay_mix, values, preferred_element_type=jnp.float32)
    return (inner_part.reshape(length, row_width), cumulative, block_state)


def per_device(
    residual_in,
    ssm_input,
    ssm_b,
    ssm_c,
    log_decay,
    skip_gain,
    out_proj,
    norm_gain,
    router,
    assignment,
    expert_gate,
    expert_up,
    expert_down,
):
    head_count = skip_gain.shape[0]
    length, row_width = ssm_input.shape
    head_size = row_width // head_count
    model_width = residual_in.shape[1]
    values = ssm_input.reshape(length, head_count, head_size)
    inner_part, cumulative, block_state = block_terms(values, ssm_b, ssm_c, log_decay)
    entry_rounded = entering(block_state, widen(jnp.exp(cumulative[-1]), row_width))
    carried = widen(jnp.exp(cumulative), row_width) * jnp.dot(
        ssm_c, entry_rounded, preferred_element_type=jnp.float32
    )
    skip_wide = widen(skip_gain, row_width)
    scan_out = (inner_part + carried + skip_wide[None, :] * ssm_input.astype(jnp.float32)).astype(
        jnp.bfloat16
    )
    mixed = residual_in.astype(jnp.float32) + jnp.dot(
        scan_out, out_proj, preferred_element_type=jnp.float32
    )
    scale = lax.rsqrt(jnp.mean(mixed * mixed, axis=1, keepdims=True) + 1e-05)
    normed = (mixed * scale * norm_gain[None, :]).astype(jnp.bfloat16)
    kernel = jnp.exp(jnp.einsum("de,td->et", router, normed, preferred_element_type=jnp.float32))
    experts = router.shape[1]
    capacity = max(16, 2 * length // experts)
    chosen = assignment[:, 0]
    hot = (chosen[:, None] == jnp.arange(experts, dtype=jnp.int32)[None, :]).astype(jnp.float32)
    upto = (jnp.arange(length)[:, None] >= jnp.arange(length)[None, :]).astype(jnp.bfloat16)
    counts = jnp.dot(upto, hot.astype(jnp.bfloat16), preferred_element_type=jnp.float32)
    slot = jnp.sum(counts * hot, axis=1).astype(jnp.int32) - 1
    position = chosen * capacity + slot
    spread = (
        position[:, None] == jnp.arange(experts * capacity, dtype=jnp.int32)[None, :]
    ).astype(jnp.bfloat16)
    packed = jnp.einsum("ts,td->sd", spread, normed, preferred_element_type=jnp.float32)
    packed = packed.astype(jnp.bfloat16).reshape(experts, capacity, model_width)
    summed, weight_row = expert_layer(
        packed, kernel, hot.T, expert_gate[0], expert_up[0], expert_down[0]
    )
    route_weight = weight_row[0]
    expert_out = jnp.dot(
        spread, summed.reshape(experts * capacity, model_width), preferred_element_type=jnp.float32
    )
    layer_out = (mixed + route_weight[:, None] * expert_out).astype(jnp.bfloat16)
    return (layer_out, route_weight)


def solution(mesh):
    in_specs = (
        P(("seq", "exp"), None),
        P(("seq", "exp"), None),
        P(("seq", "exp"), None),
        P(("seq", "exp"), None),
        P(("seq", "exp"), None),
        P(),
        P(),
        P(),
        P(),
        P(("seq", "exp"), None),
        P(("seq", "exp"), None, None),
        P(("seq", "exp"), None, None),
        P(("seq", "exp"), None, None),
    )
    out_specs = (P(("seq", "exp"), None), P(("seq", "exp")))
    return jax.shard_map(
        per_device, mesh=mesh, in_specs=in_specs, out_specs=out_specs, check_vma=False
    )
```

```python
import functools

import jax
import jax.numpy as jnp
from jax import lax
from jax.experimental import pallas as pl
from jax.experimental.pallas import tpu as pltpu
from jax.sharding import PartitionSpec as P

SINK_ITERS = 8
LANES = 128
MESH = pl.DeviceIdType.MESH


def place(flat):
    across = lax.axis_size("exp")
    return (flat // across, flat % across)


def own_index():
    return lax.axis_index("seq") * lax.axis_size("exp") + lax.axis_index("exp")


def device_count():
    return lax.axis_size("seq") * lax.axis_size("exp")


def meet_all(me, devices):
    barrier = pltpu.get_barrier_semaphore()

    @pl.loop(1, devices)
    def _(step):
        pl.semaphore_signal(
            barrier, inc=1, device_id=place((me + step) % devices), device_id_type=MESH
        )

    pl.semaphore_wait(barrier, devices - 1)


def entry_kernel(devices, pieces, src_ref, factor_ref, out_ref, arrived, entries, factors,
                 go_send, go_recv, factor_send, factor_recv, back_send, back_recv, own_sem):
    me = own_index()
    groups = out_ref.shape[1] // LANES
    rows = arrived.shape[2]

    def region(ref, flat, piece):
        return ref.at[
            pl.ds(pl.multiple_of(((flat // groups) * pieces + piece) * rows, rows), rows),
            pl.ds(pl.multiple_of((flat % groups) * LANES, LANES), LANES),
        ]

    def remote(src, dst, send, recv, peer):
        return pltpu.make_async_remote_copy(
            src_ref=src, dst_ref=dst, send_sem=send, recv_sem=recv, device_id=place(peer), device_id_type=MESH)

    def state_copy(piece, peer, slot):
        return remote(region(src_ref, peer, piece), arrived.at[piece, slot], go_send.at[piece, peer],
                      go_recv.at[piece, slot], peer)

    def factor_copy(peer, slot):
        return remote(factor_ref.at[peer % groups], factors.at[slot], factor_send.at[peer],
                      factor_recv.at[slot], peer)

    def entry_copy(piece, peer, slot):
        return remote(entries.at[piece, peer], region(out_ref, slot, piece), back_send.at[piece, peer],
                      back_recv.at[piece, slot], peer)

    own_factor = pltpu.make_async_copy(factor_ref.at[me % groups], factors.at[me], own_sem.at[0])
    own_state = [
        pltpu.make_async_copy(region(src_ref, me, piece), arrived.at[piece, me], own_sem.at[1 + piece])
        for piece in range(pieces)
    ]
    own_factor.start()
    for piece in range(pieces):
        own_state[piece].start()
    meet_all(me, devices)

    @pl.loop(1, devices)
    def _(step):
        peer = (me + step) % devices
        factor_copy(peer, me).start()
        state_copy(0, peer, me).start()

    for piece in range(1, pieces):
        @pl.loop(1, devices)
        def _(step):
            state_copy(piece, (me + step) % devices, me).start()

    own_factor.wait()
    for piece in range(pieces):
        own_state[piece].wait()

        @pl.loop(1, devices)
        def _(step):
            peer = (me + devices - step) % devices
            if piece == 0:
                factor_copy(peer, peer).wait_recv()
            state_copy(piece, peer, peer).wait_recv()

        def advance(k, state):
            entries[piece, k] = state.astype(entries.dtype)
            return factors[k] * state + arrived[piece, k].astype(jnp.float32)

        lax.fori_loop(0, devices, advance, jnp.zeros((rows, LANES), jnp.float32))

        @pl.loop(1, devices)
        def _(step):
            entry_copy(piece, (me + step) % devices, me).start()

    own_back = [
        pltpu.make_async_copy(entries.at[piece, me], region(out_ref, me, piece), own_sem.at[1 + piece])
        for piece in range(pieces)
    ]
    for piece in range(pieces):
        own_back[piece].start()

    @pl.loop(1, devices)
    def _(step):
        peer = (me + devices - step) % devices
        factor_copy(peer, peer).wait_send()
        for piece in range(pieces):
            state_copy(piece, peer, peer).wait_send()
            entry_copy(piece, peer, peer).wait_recv()
            entry_copy(piece, peer, peer).wait_send()

    for piece in range(pieces):
        own_back[piece].wait()


def entering(block_state, factor):
    devices = device_count()
    state_size, width = block_state.shape
    groups = width // LANES
    rows = state_size * groups // devices
    pieces = 2 if rows % 32 == 0 else 1
    dma = pltpu.SemaphoreType.DMA
    vmem = pl.BlockSpec(memory_space=pltpu.VMEM)
    held = pltpu.VMEM((pieces, devices, rows // pieces, LANES), jnp.bfloat16)
    each = dma((pieces, devices))
    return pl.pallas_call(
        functools.partial(entry_kernel, devices, pieces),
        out_shape=jax.ShapeDtypeStruct((state_size, width), jnp.bfloat16),
        in_specs=[vmem, vmem],
        out_specs=vmem,
        scratch_shapes=[
            held, held, pltpu.VMEM((devices, 1, LANES), jnp.float32),
            each, each, dma((devices,)), dma((devices,)), each, each, dma((1 + pieces,)),
        ],
        compiler_params=pltpu.CompilerParams(
            collective_id=0, has_side_effects=True, vmem_limit_bytes=16 << 20
        ),
        name="entry_states",
    )(block_state.astype(jnp.bfloat16), factor.reshape(groups, 1, LANES))


def expert_kernel(devices, group, packed_ref, kernel_ref, hot_ref, gate_hbm, up_hbm, down_hbm, out_ref, weight_ref,
                  table_ref, rows, halves, partial, summed, gate, up, down, block,
                  go_send, go_recv, pass_send, pass_recv, swap_send, swap_recv, back_send, back_recv,
                  near_send, near_recv, far_send, far_recv, own_sem, weight_sem):
    line, spot = lax.axis_index("seq"), lax.axis_index("exp")
    lines, spots = lax.axis_size("seq"), lax.axis_size("exp")
    me = line * spots + spot
    side, mine = me % 2, me // 2
    experts = devices // 2
    partner = me + 1 - 2 * side
    capacity, width = packed_ref.shape[1:]
    turns = experts // group

    def remote(src, dst, send, recv, device):
        return pltpu.make_async_remote_copy(
            src_ref=src, dst_ref=dst, send_sem=send, recv_sem=recv, device_id=device, device_id_type=MESH)

    def row_copy(other, slot):
        return remote(packed_ref.at[other], rows.at[side, slot], go_send.at[other], go_recv.at[slot],
                      place(2 * other + side))

    def pass_copy(at, slot):
        return remote(rows.at[side, slot], rows.at[at, slot], pass_send.at[slot], pass_recv.at[slot],
                      place(partner))

    def swap_copy(slot):
        return remote(halves.at[1 - side, slot], partial.at[slot], swap_send.at[slot], swap_recv.at[slot],
                      place(partner))

    def back_copy(other, slot):
        return remote(summed.at[other], out_ref.at[slot], back_send.at[other], back_recv.at[slot],
                      place(2 * other + side))

    def near_copy(other, slot):
        return remote(kernel_ref, table_ref.at[line, slot], near_send.at[other], near_recv.at[slot],
                      (line, other))

    def far_copy(other, slot):
        return remote(table_ref.at[line], table_ref.at[slot], far_send.at[other], far_recv.at[slot],
                      (other, spot))

    own_rows = pltpu.make_async_copy(packed_ref.at[mine], rows.at[side, mine], own_sem.at[0])
    own_table = pltpu.make_async_copy(kernel_ref, table_ref.at[line, spot], own_sem.at[1])
    own_rows.start()
    own_table.start()
    loads = [
        pltpu.make_async_copy(gate_hbm, gate, weight_sem.at[0]),
        pltpu.make_async_copy(up_hbm, up, weight_sem.at[1]),
        pltpu.make_async_copy(down_hbm, down, weight_sem.at[2]),
    ]
    for load in loads:
        load.start()
    meet_all(me, devices)

    @pl.loop(1, experts)
    def _(step):
        row_copy((mine + step) % experts, mine).start()

    @pl.loop(1, spots)
    def _(step):
        near_copy((spot + step) % spots, spot).start()

    own_rows.wait()
    pass_copy(side, mine).start()
    for load in loads:
        load.wait()

    def source_of(turn, at):
        return (mine + 2 * experts - (turn * group + at)) % experts

    @pl.loop(0, turns + 2)
    def _(turn):
        @pl.when(turn < turns)
        def _():
            @pl.loop(0, group)
            def _(at):
                @pl.when(turn * group + at > 0)
                def _():
                    source = source_of(turn, at)
                    row_copy(source, source).wait_recv()
                    pass_copy(side, source).start()

        @pl.when((turn >= 1) & (turn <= turns))
        def _():
            @pl.loop(0, group)
            def _(at):
                pass_copy(1 - side, source_of(turn - 1, at)).wait_recv()

            sources = [source_of(turn - 1, at) for at in range(group)]
            places = [(k, source, (k * group + at) * capacity)
                      for k in range(2) for at, source in enumerate(sources)]
            for k, source, start in places:
                block[start:start + capacity] = rows[k, source]
            taken = block[...]
            across = (((1,), (1,)), ((), ()))
            gate_val = lax.dot_general(taken, gate[...], across, preferred_element_type=jnp.float32)
            up_val = lax.dot_general(taken, up[...], across, preferred_element_type=jnp.float32)
            hidden = (gate_val / (1.0 + jnp.exp(-gate_val)) * up_val).astype(jnp.bfloat16)
            piece = 512
            for column in range(0, width, piece):
                made = jnp.dot(hidden, down[:, column:column + piece], preferred_element_type=jnp.float32)
                made = made.astype(halves.dtype)
                for k, source, start in places:
                    halves[k, source, :, column:column + piece] = made[start:start + capacity]

            @pl.loop(0, group)
            def _(at):
                swap_copy(source_of(turn - 1, at)).start()

        @pl.when(turn >= 2)
        def _():
            @pl.loop(0, group)
            def _(at):
                source = source_of(turn - 2, at)
                swap_copy(source).wait_recv()
                summed[source] = (
                    halves[side, source].astype(jnp.float32) + partial[source].astype(jnp.float32)
                ).astype(summed.dtype)

                @pl.when((turn - 2) * group + at > 0)
                def _():
                    back_copy(source, mine).start()

        @pl.when(turn == 1)
        def _():
            own_table.wait()

            @pl.loop(1, spots)
            def _(step):
                near_copy((spot + step) % spots, (spot + step) % spots).wait_recv()

            @pl.loop(1, lines)
            def _(step):
                far_copy((line + step) % lines, line).start()

    own_out = pltpu.make_async_copy(summed.at[mine], out_ref.at[mine], own_sem.at[0])
    own_out.start()

    @pl.loop(1, lines)
    def _(step):
        other = (line + step) % lines
        far_copy(other, other).wait_recv()
        far_copy(other, other).wait_send()

    choices, length = kernel_ref.shape

    def sweep(_, column):
        def add(at, totals):
            part = table_ref[at]
            row_scale = 1.0 / jnp.sum(part * column[None], axis=1, keepdims=True)
            return totals + jnp.sum(part * row_scale, axis=0)

        totals = lax.fori_loop(0, lines, add, jnp.zeros((choices, length), jnp.float32))
        return 1.0 / jnp.sum(totals, axis=1, keepdims=True)

    column = lax.fori_loop(0, SINK_ITERS, sweep, jnp.ones((choices, 1), jnp.float32))
    weighted = kernel_ref[...] * column
    picked = jnp.sum(jnp.where(hot_ref[...] > 0.0, weighted, 0.0), axis=0, keepdims=True)
    weight_ref[...] = choices * picked / jnp.sum(weighted, axis=0, keepdims=True)

    @pl.loop(1, spots)
    def _(step):
        near_copy((spot + step) % spots, spot).wait_send()

    @pl.loop(0, experts)
    def _(step):
        pass_copy(side, step).wait_send()
        swap_copy(step).wait_send()

    @pl.loop(1, experts)
    def _(step):
        other = (mine + step) % experts
        row_copy(other, other).wait_send()
        back_copy(other, other).wait_recv()
        back_copy(other, other).wait_send()

    own_out.wait()


def expert_layer(packed, kernel, hot, gate_half, up_half, down_half):
    devices = device_count()
    lines, spots = lax.axis_size("seq"), lax.axis_size("exp")
    experts, capacity, width = packed.shape
    hidden_units = down_half.shape[0]
    group = 8
    dma = pltpu.SemaphoreType.DMA
    vmem = pl.BlockSpec(memory_space=pltpu.VMEM)
    anywhere = pl.BlockSpec(memory_space=pl.ANY)
    single = pltpu.VMEM((experts, capacity, width), packed.dtype)
    double = pltpu.VMEM((2, experts, capacity, width), packed.dtype)
    weights = pltpu.VMEM((hidden_units, width), packed.dtype)
    each = dma((experts,))
    return pl.pallas_call(
        functools.partial(expert_kernel, devices, group),
        out_shape=(
            jax.ShapeDtypeStruct((experts, capacity, width), packed.dtype),
            jax.ShapeDtypeStruct((1, kernel.shape[1]), kernel.dtype),
        ),
        in_specs=[vmem, vmem, vmem, anywhere, anywhere, anywhere],
        out_specs=(vmem, vmem),
        scratch_shapes=[
            pltpu.VMEM((lines, spots, *kernel.shape), kernel.dtype),
            double, double, single, single, weights, weights, weights,
            pltpu.VMEM((2 * group * capacity, width), packed.dtype),
            each, each, each, each, each, each, each, each,
            dma((spots,)), dma((spots,)), dma((lines,)), dma((lines,)), dma((2,)), dma((3,)),
        ],
        compiler_params=pltpu.CompilerParams(collective_id=1, has_side_effects=True),
        name="expert_layer",
    )(packed, kernel, hot, gate_half.T, up_half.T, down_half)


def widen(per_head, width):
    return jnp.repeat(per_head, width // per_head.shape[-1], axis=-1)


def block_terms(values, b_matrix, c_matrix, decay):
    length, head_count, head_size = values.shape
    row_width = head_count * head_size
    cumulative = jnp.cumsum(decay, axis=0)
    weight = jnp.sqrt(-jnp.expm1(2.0 * decay))
    flat_values = values.reshape(length, row_width)
    tail_weight = jnp.exp(cumulative[-1:] - cumulative) * weight
    tail_in = (flat_values.astype(jnp.float32) * widen(tail_weight, row_width)).astype(jnp.bfloat16)
    block_state = jnp.einsum("sn,sc->nc", b_matrix, tail_in, preferred_element_type=jnp.float32)
    scores = jnp.einsum("tn,sn->ts", c_matrix, b_matrix, preferred_element_type=jnp.float32)
    leading = cumulative.T
    distance = leading[:, :, None] - leading[:, None, :]
    causal = jnp.arange(length)[:, None] >= jnp.arange(length)[None, :]
    decay_mix = jnp.where(causal, jnp.exp(jnp.minimum(distance, 0.0)), 0.0) * (
        weight.T[:, None, :] * scores[None, :, :]
    )
    decay_mix = decay_mix.astype(jnp.bfloat16)
    inner_part = jnp.einsum("hts,shp->thp", decay_mix, values, preferred_element_type=jnp.float32)
    return (inner_part.reshape(length, row_width), cumulative, block_state)


def per_device(
    residual_in,
    ssm_input,
    ssm_b,
    ssm_c,
    log_decay,
    skip_gain,
    out_proj,
    norm_gain,
    router,
    assignment,
    expert_gate,
    expert_up,
    expert_down,
):
    head_count = skip_gain.shape[0]
    length, row_width = ssm_input.shape
    head_size = row_width // head_count
    model_width = residual_in.shape[1]
    values = ssm_input.reshape(length, head_count, head_size)
    inner_part, cumulative, block_state = block_terms(values, ssm_b, ssm_c, log_decay)
    entry_rounded = entering(block_state, widen(jnp.exp(cumulative[-1]), row_width))
    carried = widen(jnp.exp(cumulative), row_width) * jnp.dot(
        ssm_c, entry_rounded, preferred_element_type=jnp.float32
    )
    skip_wide = widen(skip_gain, row_width)
    scan_out = (inner_part + carried + skip_wide[None, :] * ssm_input.astype(jnp.float32)).astype(
        jnp.bfloat16
    )
    mixed = residual_in.astype(jnp.float32) + jnp.dot(
        scan_out, out_proj, preferred_element_type=jnp.float32
    )
    scale = lax.rsqrt(jnp.mean(mixed * mixed, axis=1, keepdims=True) + 1e-05)
    normed = (mixed * scale * norm_gain[None, :]).astype(jnp.bfloat16)
    kernel = jnp.exp(jnp.einsum("de,td->et", router, normed, preferred_element_type=jnp.float32))
    experts = router.shape[1]
    capacity = max(16, 2 * length // experts)
    chosen = assignment[:, 0]
    hot = (chosen[:, None] == jnp.arange(experts, dtype=jnp.int32)[None, :]).astype(jnp.float32)
    upto = (jnp.arange(length)[:, None] >= jnp.arange(length)[None, :]).astype(jnp.bfloat16)
    counts = jnp.dot(upto, hot.astype(jnp.bfloat16), preferred_element_type=jnp.float32)
    slot = jnp.sum(counts * hot, axis=1).astype(jnp.int32) - 1
    position = chosen * capacity + slot
    spread = (
        position[:, None] == jnp.arange(experts * capacity, dtype=jnp.int32)[None, :]
    ).astype(jnp.bfloat16)
    packed = jnp.einsum("ts,td->sd", spread, normed, preferred_element_type=jnp.float32)
    packed = packed.astype(jnp.bfloat16).reshape(experts, capacity, model_width)
    summed, weight_row = expert_layer(
        packed, kernel, hot.T, expert_gate[0], expert_up[0], expert_down[0]
    )
    route_weight = weight_row[0]
    expert_out = jnp.dot(
        spread, summed.reshape(experts * capacity, model_width), preferred_element_type=jnp.float32
    )
    layer_out = (mixed + route_weight[:, None] * expert_out).astype(jnp.bfloat16)
    return (layer_out, route_weight)


def solution(mesh):
    in_specs = (
        P(("seq", "exp"), None),
        P(("seq", "exp"), None),
        P(("seq", "exp"), None),
        P(("seq", "exp"), None),
        P(("seq", "exp"), None),
        P(),
        P(),
        P(),
        P(),
        P(("seq", "exp"), None),
        P(("seq", "exp"), None, None),
        P(("seq", "exp"), None, None),
        P(("seq", "exp"), None, None),
    )
    out_specs = (P(("seq", "exp"), None), P(("seq", "exp")))
    return jax.shard_map(
        per_device, mesh=mesh, in_specs=in_specs, out_specs=out_specs, check_vma=False
    )
```

```python
import functools

import jax
import jax.numpy as jnp
from jax import lax
from jax.experimental import pallas as pl
from jax.experimental.pallas import tpu as pltpu
from jax.sharding import PartitionSpec as P

SINK_ITERS = 8
LANES = 128
MESH = pl.DeviceIdType.MESH


def place(flat):
    across = lax.axis_size("exp")
    return (flat // across, flat % across)


def own_index():
    return lax.axis_index("seq") * lax.axis_size("exp") + lax.axis_index("exp")


def device_count():
    return lax.axis_size("seq") * lax.axis_size("exp")


def meet_all(me, devices):
    barrier = pltpu.get_barrier_semaphore()

    @pl.loop(1, devices)
    def _(step):
        pl.semaphore_signal(
            barrier, inc=1, device_id=place((me + step) % devices), device_id_type=MESH
        )

    pl.semaphore_wait(barrier, devices - 1)


def entry_kernel(devices, pieces, src_ref, factor_ref, out_ref, arrived, entries, factors,
                 go_send, go_recv, factor_send, factor_recv, back_send, back_recv, own_sem):
    me = own_index()
    groups = out_ref.shape[1] // LANES
    rows = arrived.shape[2]

    def region(ref, flat, piece):
        return ref.at[
            pl.ds(pl.multiple_of(((flat // groups) * pieces + piece) * rows, rows), rows),
            pl.ds(pl.multiple_of((flat % groups) * LANES, LANES), LANES),
        ]

    def remote(src, dst, send, recv, peer):
        return pltpu.make_async_remote_copy(
            src_ref=src, dst_ref=dst, send_sem=send, recv_sem=recv, device_id=place(peer), device_id_type=MESH)

    def state_copy(piece, peer, slot):
        return remote(region(src_ref, peer, piece), arrived.at[piece, slot], go_send.at[piece, peer],
                      go_recv.at[piece, slot], peer)

    def factor_copy(peer, slot):
        return remote(factor_ref.at[peer % groups], factors.at[slot], factor_send.at[peer],
                      factor_recv.at[slot], peer)

    def entry_copy(piece, peer, slot):
        return remote(entries.at[piece, peer], region(out_ref, slot, piece), back_send.at[piece, peer],
                      back_recv.at[piece, slot], peer)

    own_factor = pltpu.make_async_copy(factor_ref.at[me % groups], factors.at[me], own_sem.at[0])
    own_state = [
        pltpu.make_async_copy(region(src_ref, me, piece), arrived.at[piece, me], own_sem.at[1 + piece])
        for piece in range(pieces)
    ]
    own_factor.start()
    for piece in range(pieces):
        own_state[piece].start()
    meet_all(me, devices)

    @pl.loop(1, devices)
    def _(step):
        peer = (me + step) % devices
        factor_copy(peer, me).start()
        state_copy(0, peer, me).start()

    for piece in range(1, pieces):
        @pl.loop(1, devices)
        def _(step):
            state_copy(piece, (me + step) % devices, me).start()

    own_factor.wait()
    for piece in range(pieces):
        own_state[piece].wait()

        @pl.loop(1, devices)
        def _(step):
            peer = (me + devices - step) % devices
            if piece == 0:
                factor_copy(peer, peer).wait_recv()
            state_copy(piece, peer, peer).wait_recv()

        def advance(k, state):
            entries[piece, k] = state.astype(entries.dtype)
            return factors[k] * state + arrived[piece, k].astype(jnp.float32)

        lax.fori_loop(0, devices, advance, jnp.zeros((rows, LANES), jnp.float32))

        @pl.loop(1, devices)
        def _(step):
            entry_copy(piece, (me + step) % devices, me).start()

    own_back = [
        pltpu.make_async_copy(entries.at[piece, me], region(out_ref, me, piece), own_sem.at[1 + piece])
        for piece in range(pieces)
    ]
    for piece in range(pieces):
        own_back[piece].start()

    @pl.loop(1, devices)
    def _(step):
        peer = (me + devices - step) % devices
        factor_copy(peer, peer).wait_send()
        for piece in range(pieces):
            state_copy(piece, peer, peer).wait_send()
            entry_copy(piece, peer, peer).wait_recv()
            entry_copy(piece, peer, peer).wait_send()

    for piece in range(pieces):
        own_back[piece].wait()


def entering(block_state, factor):
    devices = device_count()
    state_size, width = block_state.shape
    groups = width // LANES
    rows = state_size * groups // devices
    pieces = 2 if rows % 32 == 0 else 1
    dma = pltpu.SemaphoreType.DMA
    vmem = pl.BlockSpec(memory_space=pltpu.VMEM)
    held = pltpu.VMEM((pieces, devices, rows // pieces, LANES), jnp.bfloat16)
    each = dma((pieces, devices))
    return pl.pallas_call(
        functools.partial(entry_kernel, devices, pieces),
        out_shape=jax.ShapeDtypeStruct((state_size, width), jnp.bfloat16),
        in_specs=[vmem, vmem],
        out_specs=vmem,
        scratch_shapes=[
            held, held, pltpu.VMEM((devices, 1, LANES), jnp.float32),
            each, each, dma((devices,)), dma((devices,)), each, each, dma((1 + pieces,)),
        ],
        compiler_params=pltpu.CompilerParams(
            collective_id=0, has_side_effects=True, vmem_limit_bytes=16 << 20
        ),
        name="entry_states",
    )(block_state.astype(jnp.bfloat16), factor.reshape(groups, 1, LANES))


def expert_kernel(devices, group, packed_ref, kernel_ref, hot_ref, gate_hbm, up_hbm, down_hbm, out_ref, weight_ref,
                  table_ref, rows, halves, partial, summed, gate, up, down, block,
                  go_send, go_recv, pass_send, pass_recv, swap_send, swap_recv, back_send, back_recv,
                  near_send, near_recv, far_send, far_recv, own_sem, weight_sem):
    line, spot = lax.axis_index("seq"), lax.axis_index("exp")
    lines, spots = lax.axis_size("seq"), lax.axis_size("exp")
    me = line * spots + spot
    side, mine = me % 2, me // 2
    experts = devices // 2
    partner = me + 1 - 2 * side
    capacity, width = packed_ref.shape[1:]
    turns = experts // group

    def remote(src, dst, send, recv, device):
        return pltpu.make_async_remote_copy(
            src_ref=src, dst_ref=dst, send_sem=send, recv_sem=recv, device_id=device, device_id_type=MESH)

    def row_copy(other, slot):
        return remote(packed_ref.at[other], rows.at[side, slot], go_send.at[other], go_recv.at[slot],
                      place(2 * other + side))

    def pass_copy(at, slot):
        return remote(rows.at[side, slot], rows.at[at, slot], pass_send.at[slot], pass_recv.at[slot],
                      place(partner))

    def swap_copy(slot):
        return remote(halves.at[1 - side, slot], partial.at[slot], swap_send.at[slot], swap_recv.at[slot],
                      place(partner))

    def back_copy(other, slot):
        return remote(summed.at[other], out_ref.at[slot], back_send.at[other], back_recv.at[slot],
                      place(2 * other + side))

    def near_copy(other, slot):
        return remote(kernel_ref, table_ref.at[line, slot], near_send.at[other], near_recv.at[slot],
                      (line, other))

    def far_copy(other, slot):
        return remote(table_ref.at[line], table_ref.at[slot], far_send.at[other], far_recv.at[slot],
                      (other, spot))

    own_rows = pltpu.make_async_copy(packed_ref.at[mine], rows.at[side, mine], own_sem.at[0])
    own_table = pltpu.make_async_copy(kernel_ref, table_ref.at[line, spot], own_sem.at[1])
    own_rows.start()
    own_table.start()
    loads = [
        pltpu.make_async_copy(gate_hbm, gate, weight_sem.at[0]),
        pltpu.make_async_copy(up_hbm, up, weight_sem.at[1]),
        pltpu.make_async_copy(down_hbm, down, weight_sem.at[2]),
    ]
    for load in loads:
        load.start()
    meet_all(me, devices)

    @pl.loop(1, experts)
    def _(step):
        row_copy((mine + step) % experts, mine).start()

    @pl.loop(1, spots)
    def _(step):
        near_copy((spot + step) % spots, spot).start()

    own_rows.wait()
    pass_copy(side, mine).start()
    for load in loads:
        load.wait()

    def source_of(turn, at):
        return (mine + 2 * experts - (turn * group + at)) % experts

    @pl.loop(0, turns + 2)
    def _(turn):
        @pl.when(turn < turns)
        def _():
            @pl.loop(0, group)
            def _(at):
                @pl.when(turn * group + at > 0)
                def _():
                    source = source_of(turn, at)
                    row_copy(source, source).wait_recv()
                    pass_copy(side, source).start()

        @pl.when((turn >= 1) & (turn <= turns))
        def _():
            @pl.loop(0, group)
            def _(at):
                pass_copy(1 - side, source_of(turn - 1, at)).wait_recv()

            sources = [source_of(turn - 1, at) for at in range(group)]
            places = [(k, source, (k * group + at) * capacity)
                      for k in range(2) for at, source in enumerate(sources)]
            for k, source, start in places:
                block[start:start + capacity] = rows[k, source]
            taken = block[...]
            across = (((1,), (1,)), ((), ()))
            gate_val = lax.dot_general(taken, gate[...], across, preferred_element_type=jnp.float32)
            up_val = lax.dot_general(taken, up[...], across, preferred_element_type=jnp.float32)
            hidden = (gate_val / (1.0 + jnp.exp(-gate_val)) * up_val).astype(jnp.bfloat16)
            piece = 512
            for column in range(0, width, piece):
                made = jnp.dot(hidden, down[:, column:column + piece], preferred_element_type=jnp.float32)
                made = made.astype(halves.dtype)
                for k, source, start in places:
                    halves[k, source, :, column:column + piece] = made[start:start + capacity]

            @pl.loop(0, group)
            def _(at):
                swap_copy(source_of(turn - 1, at)).start()

        @pl.when(turn >= 2)
        def _():
            @pl.loop(0, group)
            def _(at):
                source = source_of(turn - 2, at)
                swap_copy(source).wait_recv()
                summed[source] = (
                    halves[side, source].astype(jnp.float32) + partial[source].astype(jnp.float32)
                ).astype(summed.dtype)

                @pl.when((turn - 2) * group + at > 0)
                def _():
                    back_copy(source, mine).start()

        @pl.when(turn == 1)
        def _():
            own_table.wait()

            @pl.loop(1, spots)
            def _(step):
                near_copy((spot + step) % spots, (spot + step) % spots).wait_recv()

            @pl.loop(1, lines)
            def _(step):
                far_copy((line + step) % lines, line).start()

    own_out = pltpu.make_async_copy(summed.at[mine], out_ref.at[mine], own_sem.at[0])
    own_out.start()

    @pl.loop(1, lines)
    def _(step):
        other = (line + step) % lines
        far_copy(other, other).wait_recv()
        far_copy(other, other).wait_send()

    choices, length = kernel_ref.shape

    def sweep(_, column):
        def add(at, totals):
            part = table_ref[at]
            row_scale = 1.0 / jnp.sum(part * column[None], axis=1, keepdims=True)
            return totals + jnp.sum(part * row_scale, axis=0)

        totals = lax.fori_loop(0, lines, add, jnp.zeros((choices, length), jnp.float32))
        return 1.0 / jnp.sum(totals, axis=1, keepdims=True)

    column = lax.fori_loop(0, SINK_ITERS, sweep, jnp.ones((choices, 1), jnp.float32))
    weighted = kernel_ref[...] * column
    picked = jnp.sum(jnp.where(hot_ref[...] > 0.0, weighted, 0.0), axis=0, keepdims=True)
    weight_ref[...] = choices * picked / jnp.sum(weighted, axis=0, keepdims=True)

    @pl.loop(1, spots)
    def _(step):
        near_copy((spot + step) % spots, spot).wait_send()

    @pl.loop(0, experts)
    def _(step):
        pass_copy(side, step).wait_send()
        swap_copy(step).wait_send()

    @pl.loop(1, experts)
    def _(step):
        other = (mine + step) % experts
        row_copy(other, other).wait_send()
        back_copy(other, other).wait_recv()
        back_copy(other, other).wait_send()

    own_out.wait()


def expert_layer(packed, kernel, hot, gate_half, up_half, down_half):
    devices = device_count()
    lines, spots = lax.axis_size("seq"), lax.axis_size("exp")
    experts, capacity, width = packed.shape
    hidden_units = down_half.shape[0]
    group = 8
    dma = pltpu.SemaphoreType.DMA
    vmem = pl.BlockSpec(memory_space=pltpu.VMEM)
    anywhere = pl.BlockSpec(memory_space=pl.ANY)
    single = pltpu.VMEM((experts, capacity, width), packed.dtype)
    double = pltpu.VMEM((2, experts, capacity, width), packed.dtype)
    weights = pltpu.VMEM((hidden_units, width), packed.dtype)
    each = dma((experts,))
    return pl.pallas_call(
        functools.partial(expert_kernel, devices, group),
        out_shape=(
            jax.ShapeDtypeStruct((experts, capacity, width), packed.dtype),
            jax.ShapeDtypeStruct((1, kernel.shape[1]), kernel.dtype),
        ),
        in_specs=[vmem, vmem, vmem, anywhere, anywhere, anywhere],
        out_specs=(vmem, vmem),
        scratch_shapes=[
            pltpu.VMEM((lines, spots, *kernel.shape), kernel.dtype),
            double, double, single, single, weights, weights, weights,
            pltpu.VMEM((2 * group * capacity, width), packed.dtype),
            each, each, each, each, each, each, each, each,
            dma((spots,)), dma((spots,)), dma((lines,)), dma((lines,)), dma((2,)), dma((3,)),
        ],
        compiler_params=pltpu.CompilerParams(
            collective_id=1, has_side_effects=True,
            vmem_limit_bytes=(20 << 20) + 20 * experts * capacity * width
        ),
        name="expert_layer",
    )(packed, kernel, hot, gate_half.T, up_half.T, down_half)


def widen(per_head, width):
    return jnp.repeat(per_head, width // per_head.shape[-1], axis=-1)


def block_terms(values, b_matrix, c_matrix, decay):
    length, head_count, head_size = values.shape
    row_width = head_count * head_size
    cumulative = jnp.cumsum(decay, axis=0)
    weight = jnp.sqrt(-jnp.expm1(2.0 * decay))
    flat_values = values.reshape(length, row_width)
    tail_weight = jnp.exp(cumulative[-1:] - cumulative) * weight
    tail_in = (flat_values.astype(jnp.float32) * widen(tail_weight, row_width)).astype(jnp.bfloat16)
    block_state = jnp.einsum("sn,sc->nc", b_matrix, tail_in, preferred_element_type=jnp.float32)
    scores = jnp.einsum("tn,sn->ts", c_matrix, b_matrix, preferred_element_type=jnp.float32)
    leading = cumulative.T
    distance = leading[:, :, None] - leading[:, None, :]
    causal = jnp.arange(length)[:, None] >= jnp.arange(length)[None, :]
    decay_mix = jnp.where(causal, jnp.exp(jnp.minimum(distance, 0.0)), 0.0) * (
        weight.T[:, None, :] * scores[None, :, :]
    )
    decay_mix = decay_mix.astype(jnp.bfloat16)
    inner_part = jnp.einsum("hts,shp->thp", decay_mix, values, preferred_element_type=jnp.float32)
    return (inner_part.reshape(length, row_width), cumulative, block_state)


def per_device(
    residual_in,
    ssm_input,
    ssm_b,
    ssm_c,
    log_decay,
    skip_gain,
    out_proj,
    norm_gain,
    router,
    assignment,
    expert_gate,
    expert_up,
    expert_down,
):
    head_count = skip_gain.shape[0]
    length, row_width = ssm_input.shape
    head_size = row_width // head_count
    model_width = residual_in.shape[1]
    values = ssm_input.reshape(length, head_count, head_size)
    inner_part, cumulative, block_state = block_terms(values, ssm_b, ssm_c, log_decay)
    entry_rounded = entering(block_state, widen(jnp.exp(cumulative[-1]), row_width))
    carried = widen(jnp.exp(cumulative), row_width) * jnp.dot(
        ssm_c, entry_rounded, preferred_element_type=jnp.float32
    )
    skip_wide = widen(skip_gain, row_width)
    scan_out = (inner_part + carried + skip_wide[None, :] * ssm_input.astype(jnp.float32)).astype(
        jnp.bfloat16
    )
    mixed = residual_in.astype(jnp.float32) + jnp.dot(
        scan_out, out_proj, preferred_element_type=jnp.float32
    )
    scale = lax.rsqrt(jnp.mean(mixed * mixed, axis=1, keepdims=True) + 1e-05)
    normed = (mixed * scale * norm_gain[None, :]).astype(jnp.bfloat16)
    kernel = jnp.exp(jnp.einsum("de,td->et", router, normed, preferred_element_type=jnp.float32))
    experts = router.shape[1]
    capacity = max(16, 2 * length // experts)
    chosen = assignment[:, 0]
    hot = (chosen[:, None] == jnp.arange(experts, dtype=jnp.int32)[None, :]).astype(jnp.float32)
    upto = (jnp.arange(length)[:, None] >= jnp.arange(length)[None, :]).astype(jnp.bfloat16)
    counts = jnp.dot(upto, hot.astype(jnp.bfloat16), preferred_element_type=jnp.float32)
    slot = jnp.sum(counts * hot, axis=1).astype(jnp.int32) - 1
    position = chosen * capacity + slot
    spread = (
        position[:, None] == jnp.arange(experts * capacity, dtype=jnp.int32)[None, :]
    ).astype(jnp.bfloat16)
    packed = jnp.einsum("ts,td->sd", spread, normed, preferred_element_type=jnp.float32)
    packed = packed.astype(jnp.bfloat16).reshape(experts, capacity, model_width)
    summed, weight_row = expert_layer(
        packed, kernel, hot.T, expert_gate[0], expert_up[0], expert_down[0]
    )
    route_weight = weight_row[0]
    expert_out = jnp.dot(
        spread, summed.reshape(experts * capacity, model_width), preferred_element_type=jnp.float32
    )
    layer_out = (mixed + route_weight[:, None] * expert_out).astype(jnp.bfloat16)
    return (layer_out, route_weight)


def solution(mesh):
    in_specs = (
        P(("seq", "exp"), None),
        P(("seq", "exp"), None),
        P(("seq", "exp"), None),
        P(("seq", "exp"), None),
        P(("seq", "exp"), None),
        P(),
        P(),
        P(),
        P(),
        P(("seq", "exp"), None),
        P(("seq", "exp"), None, None),
        P(("seq", "exp"), None, None),
        P(("seq", "exp"), None, None),
    )
    out_specs = (P(("seq", "exp"), None), P(("seq", "exp")))
    return jax.shard_map(
        per_device, mesh=mesh, in_specs=in_specs, out_specs=out_specs, check_vma=False
    )
```
